32 devices in a mesh: rep: 2 (over x), grp: 8 (over z, y), mem: 2 (over core).
Axes of the slice: x: 2, y: 2, z: 4, core: 2. Of those that a mesh axis runs over, the one named last changes fastest.
Arguments:
- layer_input: bfloat16 [4096, 2048], P(('rep', 'grp', 'mem')), parts along dimension 0, may hold values from -6 to 6
- output_grad: bfloat16 [4096, 2048], P(('rep', 'grp', 'mem')), parts along dimension 0, may hold values from -24 to 24
- expert_ids: int32 [4096, 8], P(('rep', 'grp', 'mem')), parts along dimension 0, may hold values from 0 to 15, all different within a row; in each aligned block of 128 rows (0 to 127, 128 to 255, ...) at most 72 rows name the same one
- route_ints: int32 [4096, 8], P(('rep', 'grp', 'mem')), parts along dimension 0, may hold values from 1 to 255
- w_gate: bfloat16 [16, 2048, 384], P(('grp', 'mem')), may hold values from -0.125 to 0.125
- w_up: bfloat16 [16, 2048, 384], P(('grp', 'mem')), may hold values from -0.125 to 0.125
- w_down: bfloat16 [16, 384, 2048], P(('grp', 'mem')), may hold values from -0.3125 to 0.3125
Outputs:
- input_grad: bfloat16 [4096, 2048], P(('rep', 'grp', 'mem')), parts along dimension 0
- grad_gate: bfloat16 [32, 2048, 384], P(('rep', 'grp', 'mem')), parts along dimension 0
- grad_up: bfloat16 [32, 2048, 384], P(('rep', 'grp', 'mem')), parts along dimension 0
- grad_down: bfloat16 [32, 384, 2048], P(('rep', 'grp', 'mem')), parts along dimension 0
The draws below stay inside these ranges and needn't reach their ends.
There are 2 independent parts, one for each index of `rep`. The reference program is written for one: setup_inputs(seed, part) draws one part's arguments, and reference() takes and returns one part's arrays. A program takes and returns all parts, laid end to end along the dimension named above; an argument that names none is the same for every part. Nothing has to cross between parts.
Inputs may be any that keep to these rules, and one draw needn't show every extreme that they name: `expert_ids`: each row names 8 different experts. The 128 rows of one device name any one expert at most 72 times, and in every draw some device names some expert exactly 72 times.
All inputs are finite; a program needn't handle non-finite values.
Results may differ from the reference program's by a relative error of at most 0.0064.
Values may be sent and summed in bfloat16 or wider, within the bound.
No kernel may reach another device: no remote copies, remote signals or barrier semaphores. Data moves between devices by JAX's collectives and lax.ppermute only.
A program may use at most 128 MiB of HBM per device.

```python
import math
import jax
import jax.numpy as jnp
import numpy as np
from jax import lax

D = 2048
FF = 384
TOP = 8
TOK_DEV = 128
EXPERTS = 16
TOKENS = 2048
CAP = 72
N_GRP = 8
N_MEM = 2


def plant(array, own_key, low, largest):
    index_at = [jax.random.randint(jax.random.fold_in(own_key, axis), (), 0, length) for axis, length in enumerate(array.shape)]
    longest = array.shape.index(max(array.shape))
    neighbour = index_at[:longest] + [(index_at[longest] + 1) % array.shape[longest]] + index_at[longest + 1:]
    return array.at[tuple(index_at)].set(low).at[tuple(neighbour)].set(largest)


def levels(rng, extent, split, low, high):
    factor_of = 1.0
    for dim, blocks in split:
        steps = jax.random.uniform(jax.random.fold_in(jax.random.fold_in(rng, 6), dim), (blocks,), jnp.float32, low / len(split), high / len(split))
        factor_of = factor_of * jnp.repeat(jnp.exp(steps), extent[dim] // blocks).reshape((-1,) + (1,) * (len(extent) - 1 - dim))
    return factor_of


def assign_block(stream_key, own, number, rows, count, top, limit, slope):
    order = jax.random.permutation(stream_key, count)
    packed, common = portions_of(count, rows * top, limit, slope, True), portions_of(count, rows * top, limit, slope, False)
    places = jnp.arange(count)

    def named(sizes, rotation):
        used = int((sizes > 0).sum())
        fixed = max(1, used // 4)
        moved = fixed + (places - fixed + rotation * (used - fixed)) % max(1, count - fixed)
        return jnp.zeros((count,), jnp.int32).at[order[jnp.where(places < fixed, places, moved)]].set(jnp.asarray(sizes, jnp.int32))

    sizes = jnp.where(number % 4 == 0, named(packed, number // 4), named(common, number - number // 4 - 1))
    mixed = jax.random.permutation(jax.random.fold_in(own, 3), count)
    donor, receiver = mixed[0:count // 2 * 2:2], mixed[1:count // 2 * 2:2]
    margin = jnp.minimum(sizes[donor] - 1, limit - sizes[receiver]) // 2
    margin = jnp.where((donor == order[0]) | (receiver == order[0]) | (sizes[receiver] == 0), 0, jnp.maximum(margin, 0))
    moved = jax.random.randint(jax.random.fold_in(own, 4), (count // 2,), 0, 1 << 20) % (margin + 1)
    sizes = sizes.at[donor].add(-moved).at[receiver].add(moved)
    labels = jnp.searchsorted(jnp.cumsum(sizes), jnp.arange(rows * top), side="right").astype(jnp.int32)
    listing = labels.reshape(top, rows).T
    listing = listing[jax.random.permutation(jax.random.fold_in(own, 1), rows)]
    rotation = jax.random.randint(jax.random.fold_in(own, 2), (rows, 1), 0, top)
    return jnp.take_along_axis(listing, (jnp.arange(top)[None, :] + rotation) % top, axis=1)


def portions_of(number_of, total, bound, lean, full):
    weights = [(1 << 20) // math.isqrt(rank ** lean) + 1 for rank in range(1, number_of + 1)]
    largest = bound if full else min(bound, max(-(-total // number_of), total * weights[0] // sum(weights)))
    least = 1 if total - largest >= number_of - 1 else 0
    holding, rest = [largest] + [least] * (number_of - 1), total - largest - least * (number_of - 1)
    while rest > 0:
        candidates = [i for i in range(1, number_of) if holding[i] < largest] or [i for i in range(1, number_of) if holding[i] < bound]
        pool, remaining = sum([weights[i] for i in candidates]), rest
        for i in candidates:
            more = min(bound - holding[i], max(1, remaining * weights[i] // pool), rest)
            holding[i] = holding[i] + more
            rest = rest - more
    return np.array(holding)


def scatter_about(stream_key, extent, width, reach, split=(), held_as=jnp.bfloat16):
    drawn = jax.random.normal(stream_key, extent, jnp.float32) * width
    if len(split) > 0:
        drawn = levels(stream_key, extent, split, -0.22, 0.18) * drawn
    return jnp.clip(drawn, min=-reach, max=reach).astype(held_as)


def setup_inputs(seed: int = 0, part: int = 0) -> dict:
    keys = jax.random.split(jax.random.key(seed), 8)
    part_keys = jax.random.split(jax.random.fold_in(keys[7], part), 8)
    layer_input = scatter_about(part_keys[0], (TOKENS, D), 1.0, 6.0, ((0, 16),))
    output_grad = scatter_about(part_keys[1], (TOKENS, D), 4.0, 24.0, ((0, 16),))
    expert_ids_keys = jax.random.split(jax.random.fold_in(part_keys[2], 1), TOKENS // TOK_DEV)
    expert_ids_turns = jax.random.permutation(jax.random.fold_in(part_keys[2], 3), TOKENS // TOK_DEV)
    expert_ids = jax.vmap(lambda own, number: assign_block(jax.random.fold_in(part_keys[2], 2), own, number, TOK_DEV, EXPERTS, TOP, CAP, 2))(expert_ids_keys, expert_ids_turns).reshape((TOKENS, TOP))
    route_ints = plant(jax.random.randint(part_keys[3], (TOKENS, TOP), 1, 256), jax.random.fold_in(part_keys[3], 1), 1, 255).astype(jnp.int32)
    w_gate = scatter_about(keys[4], (EXPERTS, D, FF), D ** -0.5, 0.125, ((0, 16),))
    w_up = scatter_about(keys[5], (EXPERTS, D, FF), D ** -0.5, 0.125, ((0, 16),))
    w_down = scatter_about(keys[6], (EXPERTS, FF, D), FF ** -0.5, 0.3125, ((0, 16),))
    return dict(layer_input=layer_input, output_grad=output_grad, expert_ids=expert_ids, route_ints=route_ints, w_gate=w_gate, w_up=w_up, w_down=w_down)


def reference(layer_input, output_grad, expert_ids, route_ints, w_gate, w_up, w_down):
    tokens = layer_input.shape[0]
    top_count = expert_ids.shape[1]
    pair_count = tokens * top_count
    quotas = route_ints.astype(jnp.float32)
    route_ratio = quotas / jnp.sum(quotas, axis=1, keepdims=True)
    scaled = (route_ratio[:, :, None] * output_grad.astype(jnp.float32)[:, None, :]).astype(jnp.bfloat16)
    scaled = scaled.reshape(pair_count, layer_input.shape[1])
    flat_ids = expert_ids.reshape(pair_count)
    most_rows = N_GRP * N_MEM * CAP

    def per_expert(grad_total, expert):
        picked = jnp.nonzero(flat_ids == expert, size=most_rows, fill_value=pair_count)[0].astype(jnp.int32)
        is_live = picked < pair_count
        safe_pick = jnp.where(is_live, picked, 0).astype(jnp.int32)
        token_index = (safe_pick // top_count).astype(jnp.int32)
        rows_x = jnp.where(is_live[:, None], layer_input[token_index], jnp.zeros((), jnp.bfloat16))
        rows_grad = jnp.where(is_live[:, None], scaled[safe_pick], jnp.zeros((), jnp.bfloat16))
        gate_w = w_gate[expert]
        up_w = w_up[expert]
        down_w = w_down[expert]
        gate_pre = jnp.dot(rows_x, gate_w, preferred_element_type=jnp.float32)
        up_pre = jnp.dot(rows_x, up_w, preferred_element_type=jnp.float32)
        sigmoid_gate = jax.nn.sigmoid(gate_pre)
        activity = gate_pre * sigmoid_gate
        hidden = (activity * up_pre).astype(jnp.bfloat16)
        hidden_grad = jnp.dot(rows_grad, down_w.T, preferred_element_type=jnp.float32)
        up_grad = (hidden_grad * activity).astype(jnp.bfloat16)
        gate_grad = (hidden_grad * up_pre * sigmoid_gate * (1.0 + gate_pre * (1.0 - sigmoid_gate))).astype(jnp.bfloat16)
        down_wgrad = jnp.dot(hidden.T, rows_grad, preferred_element_type=jnp.float32).astype(jnp.bfloat16)
        gate_wgrad = jnp.dot(rows_x.T, gate_grad, preferred_element_type=jnp.float32).astype(jnp.bfloat16)
        up_wgrad = jnp.dot(rows_x.T, up_grad, preferred_element_type=jnp.float32).astype(jnp.bfloat16)
        row_grad = (jnp.dot(gate_grad, gate_w.T, preferred_element_type=jnp.float32)
                    + jnp.dot(up_grad, up_w.T, preferred_element_type=jnp.float32)).astype(jnp.bfloat16)
        target = jnp.where(is_live, token_index, tokens).astype(jnp.int32)
        grad_total = grad_total.at[target].add(row_grad.astype(jnp.float32), mode="drop")
        return grad_total, (gate_wgrad, up_wgrad, down_wgrad)

    start_total = jnp.zeros(layer_input.shape, jnp.float32)
    grad_total, stacked = lax.scan(per_expert, start_total, jnp.arange(EXPERTS, dtype=jnp.int32))
    return grad_total.astype(jnp.bfloat16), stacked[0], stacked[1], stacked[2]
```

```python
import jax
import jax.numpy as jnp
from jax import lax
from jax.sharding import PartitionSpec as P


def exchange_plan(layer_input, output_grad, expert_ids, route_ints, w_gate, w_up, w_down):
    devices = lax.axis_size("grp") * lax.axis_size("mem")
    tok_rows = layer_input.shape[0]
    model_width = layer_input.shape[1]
    top_count = expert_ids.shape[1]
    pair_count = tok_rows * top_count
    capacity = max(2, 9 * tok_rows * top_count // (8 * devices))
    slot_count = devices * capacity
    quotas = route_ints.astype(jnp.float32)
    route_ratio = quotas / jnp.sum(quotas, axis=1, keepdims=True)
    scaled = (route_ratio[:, :, None] * output_grad.astype(jnp.float32)[:, None, :]).astype(
        jnp.bfloat16
    )
    scaled = scaled.reshape(pair_count, model_width)
    flat_ids = expert_ids.reshape(pair_count)
    pair_order = jnp.arange(pair_count, dtype=jnp.int32)
    earlier = (flat_ids[None, :] == flat_ids[:, None]) & (pair_order[None, :] < pair_order[:, None])
    slot_rank = jnp.sum(earlier.astype(jnp.int32), axis=1)
    slot_key = flat_ids * capacity + slot_rank
    slot_match = slot_key[None, :] == jnp.arange(slot_count, dtype=jnp.int32)[:, None]
    filled = jnp.any(slot_match, axis=1)
    source_pair = jnp.sum(jnp.where(slot_match, pair_order[None, :], 0), axis=1)
    send_x = jnp.where(
        filled[:, None], layer_input[source_pair // top_count], jnp.zeros((), jnp.bfloat16)
    )
    send_grad = jnp.where(filled[:, None], scaled[source_pair], jnp.zeros((), jnp.bfloat16))
    recv_x, recv_grad = (
        lax.all_to_all(
            send_x.reshape(devices, capacity, model_width),
            ("grp", "mem"),
            split_axis=0,
            concat_axis=0,
            tiled=True,
        ),
        lax.all_to_all(
            send_grad.reshape(devices, capacity, model_width),
            ("grp", "mem"),
            split_axis=0,
            concat_axis=0,
            tiled=True,
        ),
    )
    rows_x = recv_x.reshape(slot_count, model_width)
    rows_grad = recv_grad.reshape(slot_count, model_width)
    gate_w = w_gate[0]
    up_w = w_up[0]
    down_w = w_down[0]
    gate_pre = jnp.dot(rows_x, gate_w, preferred_element_type=jnp.float32)
    up_pre = jnp.dot(rows_x, up_w, preferred_element_type=jnp.float32)
    sigmoid_gate = jax.nn.sigmoid(gate_pre)
    activity = gate_pre * sigmoid_gate
    hidden = (activity * up_pre).astype(jnp.bfloat16)
    hidden_grad = jnp.dot(rows_grad, down_w.T, preferred_element_type=jnp.float32)
    up_grad = (hidden_grad * activity).astype(jnp.bfloat16)
    gate_grad = (
        hidden_grad * up_pre * sigmoid_gate * (1.0 + gate_pre * (1.0 - sigmoid_gate))
    ).astype(jnp.bfloat16)
    row_grad = (
        jnp.dot(gate_grad, gate_w.T, preferred_element_type=jnp.float32)
        + jnp.dot(up_grad, up_w.T, preferred_element_type=jnp.float32)
    ).astype(jnp.bfloat16)
    returned = lax.all_to_all(
        row_grad.reshape(devices, capacity, model_width),
        ("grp", "mem"),
        split_axis=0,
        concat_axis=0,
        tiled=True,
    )
    down_wgrad = jnp.dot(hidden.T, rows_grad, preferred_element_type=jnp.float32).astype(
        jnp.bfloat16
    )
    gate_wgrad = jnp.dot(rows_x.T, gate_grad, preferred_element_type=jnp.float32).astype(
        jnp.bfloat16
    )
    up_wgrad = jnp.dot(rows_x.T, up_grad, preferred_element_type=jnp.float32).astype(jnp.bfloat16)
    back_rows = returned.reshape(slot_count, model_width)
    pair_rows = back_rows[slot_key].reshape(tok_rows, top_count, model_width)
    input_grad = jnp.sum(pair_rows.astype(jnp.float32), axis=1).astype(jnp.bfloat16)
    return (input_grad, gate_wgrad[None], up_wgrad[None], down_wgrad[None])


def ring_order(count):
    return list(range(0, count, 2)) + list(reversed(range(1, count, 2)))


def ring_plan(layer_input, output_grad, expert_ids, route_ints, w_gate, w_up, w_down):
    groups = lax.axis_size("grp")
    members = lax.axis_size("mem")
    tok_rows, model_width = layer_input.shape
    hidden_width = w_gate.shape[2]
    order = ring_order(groups)
    right = [(order[i], order[(i + 1) % groups]) for i in range(groups)]
    left = [(b, a) for a, b in right]
    place_of = [order.index(g) for g in range(groups)]
    spot = jnp.array(place_of, jnp.int32)[lax.axis_index("grp")]
    member = lax.axis_index("mem")

    def shift(array, direction):
        return lax.ppermute(array, "grp", direction)

    def member_shift(array, step):
        return lax.ppermute(array, "mem", [(m, (m + step) % members) for m in range(members)])

    full_steps = (groups - 1) // 2
    has_far = groups % 2 == 0 and groups > 1
    from_left, from_right = [], []
    rx, rg, lx, lg = layer_input, output_grad, layer_input, output_grad
    for _ in range(full_steps):
        rx, lx = shift(rx, right), shift(lx, left)
        rg, lg = shift(rg, right), shift(lg, left)
        from_left.append((rx, rg))
        from_right.append((lx, lg))
    far = (shift(rx, right), shift(lg, left)) if has_far else None

    quotas = route_ints.astype(jnp.float32)
    route_ratio = quotas / jnp.sum(quotas, axis=1, keepdims=True)
    experts = groups * members
    one_hot = expert_ids[:, None, :] == jnp.arange(experts, dtype=jnp.int32)[None, :, None]
    ratio_by_expert = jnp.sum(jnp.where(one_hot, route_ratio[:, None, :], 0.0), axis=2)
    outgoing = ratio_by_expert.T.reshape(groups, members, tok_rows)
    incoming = lax.all_to_all(outgoing, "grp", split_axis=0, concat_axis=0, tiled=True)
    incoming = jnp.stack(
        [
            lax.dynamic_index_in_dim(incoming, (member + k) % members, 1, keepdims=False)
            for k in range(members)
        ],
        axis=1,
    )
    order_table = jnp.array(order, jnp.int32)

    def ratios_at(distance):
        source = order_table[(spot + distance) % groups]
        return lax.dynamic_index_in_dim(incoming, source, 0, keepdims=False)

    gates, ups, downs = [w_gate[0]], [w_up[0]], [w_down[0]]
    for k in range(1, members):
        gates.append(member_shift(w_gate[0], members - k))
        ups.append(member_shift(w_up[0], members - k))
        downs.append(member_shift(w_down[0], members - k))
    w_in = jnp.concatenate(gates + ups, axis=1)
    w_out = jnp.concatenate(downs, axis=0)
    span = members * hidden_width

    def piece(x, og, ratio):
        r = jnp.repeat(ratio.T, hidden_width, axis=1)
        pre = jnp.dot(x, w_in, preferred_element_type=jnp.float32)
        gate, up = pre[:, :span], pre[:, span:]
        s = jax.nn.sigmoid(gate)
        act = gate * s
        hidden = (act * up * r).astype(jnp.bfloat16)
        hg = r * lax.dot_general(
            og, w_out, (((1,), (1,)), ((), ())), preferred_element_type=jnp.float32
        )
        ug = (hg * act).astype(jnp.bfloat16)
        gg = (hg * up * s * (1.0 + gate * (1.0 - s))).astype(jnp.bfloat16)
        grads = jnp.concatenate([gg, ug], axis=1)
        part = lax.dot_general(
            grads, w_in, (((1,), (1,)), ((), ())), preferred_element_type=jnp.float32
        )
        return part, grads, hidden

    xs, ogs, all_grads, all_hidden = [], [], [], []

    def record(x, og, grads, hidden):
        xs.append(x)
        ogs.append(og)
        all_grads.append(grads)
        all_hidden.append(hidden)

    own_part, grads, hidden = piece(layer_input, output_grad, ratios_at(0))
    record(layer_input, output_grad, grads, hidden)
    part_left, part_right = [], []
    for k in range(1, full_steps + 1):
        x = jnp.concatenate([from_left[k - 1][0], from_right[k - 1][0]], axis=0)
        og = jnp.concatenate([from_left[k - 1][1], from_right[k - 1][1]], axis=0)
        ratio = jnp.concatenate([ratios_at(-k), ratios_at(k)], axis=1)
        part, grads, hidden = piece(x, og, ratio)
        part = part.astype(jnp.bfloat16)
        part_left.append(part[:tok_rows])
        part_right.append(part[tok_rows:])
        record(x, og, grads, hidden)
    half = tok_rows // 2
    far_part = None
    if has_far:
        part, grads, hidden = piece(far[0], far[1], ratios_at(groups // 2))
        far_part = part.astype(jnp.bfloat16)
        record(far[0], far[1], grads, hidden)

    def travel(parts, far_rows, rows, direction):
        running = far_rows
        for k in reversed(range(full_steps)):
            mine = parts[k][rows]
            if running is not None:
                moved = shift(running, direction)
                mine = (moved.astype(jnp.float32) + mine.astype(jnp.float32)).astype(jnp.bfloat16)
            running = mine
        return None if running is None else shift(running, direction)

    low, high = slice(0, half), slice(half, tok_rows)
    back_low = [
        travel(part_left, far_part[low] if has_far else None, low, left),
        travel(part_right, None, low, right),
    ]
    back_high = [
        travel(part_left, None, high, left),
        travel(part_right, far_part[high] if has_far else None, high, right),
    ]

    def closing(rows, returned):
        total = own_part[rows]
        for piece_back in returned:
            if piece_back is not None:
                total = total + piece_back.astype(jnp.float32)
        return total.astype(jnp.bfloat16)

    input_grad = jnp.concatenate([closing(low, back_low), closing(high, back_high)], axis=0)

    x_all, og_all = jnp.concatenate(xs, axis=0), jnp.concatenate(ogs, axis=0)
    grads_all = jnp.concatenate(all_grads, axis=0)
    hidden_all = jnp.concatenate(all_hidden, axis=0)
    down_w = lax.dot_general(
        hidden_all, og_all, (((0,), (0,)), ((), ())), preferred_element_type=jnp.float32
    )
    in_w = lax.dot_general(
        x_all, grads_all, (((0,), (0,)), ((), ())), preferred_element_type=jnp.float32
    )

    def gather_members(blocks):
        total = blocks[0]
        for k in range(1, members):
            total = total + member_shift(blocks[k].astype(jnp.bfloat16), k).astype(jnp.float32)
        return total.astype(jnp.bfloat16)[None]

    width = hidden_width
    down_g = gather_members([down_w[k * width : (k + 1) * width] for k in range(members)])
    gate_g = gather_members([in_w[:, k * width : (k + 1) * width] for k in range(members)])
    up_g = gather_members(
        [in_w[:, span + k * width : span + (k + 1) * width] for k in range(members)]
    )
    return (input_grad, gate_g, up_g, down_g)


def local(layer_input, output_grad, expert_ids, route_ints, w_gate, w_up, w_down):
    devices = lax.axis_size("grp") * lax.axis_size("mem")
    tok_rows, top_count = expert_ids.shape
    capacity = max(2, 9 * tok_rows * top_count // (8 * devices))
    plan = ring_plan if tok_rows <= 2 * capacity else exchange_plan
    return plan(layer_input, output_grad, expert_ids, route_ints, w_gate, w_up, w_down)


def solution(mesh):
    return jax.shard_map(
        local,
        mesh=mesh,
        in_specs=(
            P(("rep", "grp", "mem"), None),
            P(("rep", "grp", "mem"), None),
            P(("rep", "grp", "mem"), None),
            P(("rep", "grp", "mem"), None),
            P(("grp", "mem"), None, None),
            P(("grp", "mem"), None, None),
            P(("grp", "mem"), None, None),
        ),
        out_specs=(
            P(("rep", "grp", "mem"), None),
            P(("rep", "grp", "mem"), None, None),
            P(("rep", "grp", "mem"), None, None),
            P(("rep", "grp", "mem"), None, None),
        ),
        check_vma=False,
    )
```

```python
import jax
import jax.numpy as jnp
from jax import lax
from jax.sharding import PartitionSpec as P


def exchange_plan(layer_input, output_grad, expert_ids, route_ints, w_gate, w_up, w_down):
    devices = lax.axis_size("grp") * lax.axis_size("mem")
    tok_rows = layer_input.shape[0]
    model_width = layer_input.shape[1]
    top_count = expert_ids.shape[1]
    pair_count = tok_rows * top_count
    capacity = max(2, 9 * tok_rows * top_count // (8 * devices))
    slot_count = devices * capacity
    quotas = route_ints.astype(jnp.float32)
    route_ratio = quotas / jnp.sum(quotas, axis=1, keepdims=True)
    scaled = (route_ratio[:, :, None] * output_grad.astype(jnp.float32)[:, None, :]).astype(
        jnp.bfloat16
    )
    scaled = scaled.reshape(pair_count, model_width)
    flat_ids = expert_ids.reshape(pair_count)
    pair_order = jnp.arange(pair_count, dtype=jnp.int32)
    earlier = (flat_ids[None, :] == flat_ids[:, None]) & (pair_order[None, :] < pair_order[:, None])
    slot_rank = jnp.sum(earlier.astype(jnp.int32), axis=1)
    slot_key = flat_ids * capacity + slot_rank
    slot_match = slot_key[None, :] == jnp.arange(slot_count, dtype=jnp.int32)[:, None]
    filled = jnp.any(slot_match, axis=1)
    source_pair = jnp.sum(jnp.where(slot_match, pair_order[None, :], 0), axis=1)
    send_x = jnp.where(
        filled[:, None], layer_input[source_pair // top_count], jnp.zeros((), jnp.bfloat16)
    )
    send_grad = jnp.where(filled[:, None], scaled[source_pair], jnp.zeros((), jnp.bfloat16))
    recv_x, recv_grad = (
        lax.all_to_all(
            send_x.reshape(devices, capacity, model_width),
            ("grp", "mem"),
            split_axis=0,
            concat_axis=0,
            tiled=True,
        ),
        lax.all_to_all(
            send_grad.reshape(devices, capacity, model_width),
            ("grp", "mem"),
            split_axis=0,
            concat_axis=0,
            tiled=True,
        ),
    )
    rows_x = recv_x.reshape(slot_count, model_width)
    rows_grad = recv_grad.reshape(slot_count, model_width)
    gate_w = w_gate[0]
    up_w = w_up[0]
    down_w = w_down[0]
    gate_pre = jnp.dot(rows_x, gate_w, preferred_element_type=jnp.float32)
    up_pre = jnp.dot(rows_x, up_w, preferred_element_type=jnp.float32)
    sigmoid_gate = jax.nn.sigmoid(gate_pre)
    activity = gate_pre * sigmoid_gate
    hidden = (activity * up_pre).astype(jnp.bfloat16)
    hidden_grad = jnp.dot(rows_grad, down_w.T, preferred_element_type=jnp.float32)
    up_grad = (hidden_grad * activity).astype(jnp.bfloat16)
    gate_grad = (
        hidden_grad * up_pre * sigmoid_gate * (1.0 + gate_pre * (1.0 - sigmoid_gate))
    ).astype(jnp.bfloat16)
    row_grad = (
        jnp.dot(gate_grad, gate_w.T, preferred_element_type=jnp.float32)
        + jnp.dot(up_grad, up_w.T, preferred_element_type=jnp.float32)
    ).astype(jnp.bfloat16)
    returned = lax.all_to_all(
        row_grad.reshape(devices, capacity, model_width),
        ("grp", "mem"),
        split_axis=0,
        concat_axis=0,
        tiled=True,
    )
    down_wgrad = jnp.dot(hidden.T, rows_grad, preferred_element_type=jnp.float32).astype(
        jnp.bfloat16
    )
    gate_wgrad = jnp.dot(rows_x.T, gate_grad, preferred_element_type=jnp.float32).astype(
        jnp.bfloat16
    )
    up_wgrad = jnp.dot(rows_x.T, up_grad, preferred_element_type=jnp.float32).astype(jnp.bfloat16)
    back_rows = returned.reshape(slot_count, model_width)
    pair_rows = back_rows[slot_key].reshape(tok_rows, top_count, model_width)
    input_grad = jnp.sum(pair_rows.astype(jnp.float32), axis=1).astype(jnp.bfloat16)
    return (input_grad, gate_wgrad[None], up_wgrad[None], down_wgrad[None])


TN = (((0,), (0,)), ((), ()))
NT = (((1,), (1,)), ((), ()))


def ring_order(count):
    return list(range(0, count, 2)) + list(reversed(range(1, count, 2)))


def mm(a, b, dims=(((1,), (0,)), ((), ()))):
    return lax.dot_general(a, b, dims, preferred_element_type=jnp.float32)


def ring_plan(layer_input, output_grad, expert_ids, route_ints, w_gate, w_up, w_down):
    groups = lax.axis_size("grp")
    members = lax.axis_size("mem")
    tok_rows, _ = layer_input.shape
    width = w_gate.shape[2]
    span = members * width
    order = ring_order(groups)
    full_steps = (groups - 1) // 2
    has_far = groups % 2 == 0 and groups > 1

    def at_distance(k):
        return [(order[i], order[(i + k) % groups]) for i in range(groups)]

    def shift(array, k):
        return lax.ppermute(array, "grp", at_distance(k))

    def member_shift(array, step):
        return lax.ppermute(array, "mem", [(m, (m + step) % members) for m in range(members)])

    from_left, from_right = [], []
    rx, rg, lx, lg = layer_input, output_grad, layer_input, output_grad
    for _ in range(1, full_steps + 1):
        rg, lg = shift(rg, 1), shift(lg, -1)
        rx, lx = shift(rx, 1), shift(lx, -1)
        from_left.append((rx, rg))
        from_right.append((lx, lg))
    far = (shift(rx, 1), shift(lg, -1)) if has_far else None

    quotas = route_ints.astype(jnp.float32)
    route_ratio = quotas / jnp.sum(quotas, axis=1, keepdims=True)
    group_at = jnp.array(
        [[order[(order.index(g) + k) % groups] for k in range(groups)] for g in range(groups)],
        jnp.int32,
    )
    mine = jnp.arange(groups, dtype=jnp.int32)[:, None] == lax.axis_index("grp")
    chip = jnp.sum(jnp.where(mine, group_at, 0), axis=0)
    core = (lax.axis_index("mem") + jnp.arange(members, dtype=jnp.int32)) % members
    expert = chip[:, None] * members + core[None, :]
    chosen = expert_ids[None, None, :, :] == expert[:, :, None, None]
    outgoing = jnp.sum(jnp.where(chosen, route_ratio[None, None], 0.0), axis=3)
    distances = [0]
    for k in range(1, full_steps + 1):
        distances += [-k, k]
    if has_far:
        distances.append(groups // 2)
    ratios = []
    for d in distances:
        ratios.append(outgoing[0] if d == 0 else shift(outgoing[(-d) % groups], -d))
    ratios = jnp.concatenate(ratios, axis=1).T

    gates, ups, downs = [w_gate[0]], [w_up[0]], [w_down[0]]
    for k in range(1, members):
        gates.append(member_shift(w_gate[0], members - k))
        ups.append(member_shift(w_up[0], members - k))
        downs.append(member_shift(w_down[0], members - k))
    gate_w = jnp.concatenate(gates, axis=1)
    up_w = jnp.concatenate(ups, axis=1)
    down_w = jnp.concatenate(downs, axis=0)
    column = jnp.arange(span, dtype=jnp.int32)[None, :] // width

    def piece(x, og, ratio):
        r = ratio[:, 0:1]
        for m in range(1, members):
            r = jnp.where(column == m, ratio[:, m : m + 1], r)
        gate, up = mm(x, gate_w), mm(x, up_w)
        s = jax.nn.sigmoid(gate)
        act = gate * s
        hidden = (act * up * r).astype(jnp.bfloat16)
        hg = r * mm(og, down_w, NT)
        ug = (hg * act).astype(jnp.bfloat16)
        gg = (hg * up * s * (1.0 + gate * (1.0 - s))).astype(jnp.bfloat16)
        part = mm(gg, gate_w, NT) + mm(ug, up_w, NT)
        return part, gg, ug, hidden

    kept = []
    own_part, *rest = piece(layer_input, output_grad, ratios[:tok_rows])
    kept.append((layer_input, output_grad, *rest))
    part_left, part_right = [], []
    at = tok_rows
    for k in range(1, full_steps + 1):
        x = jnp.concatenate([from_left[k - 1][0], from_right[k - 1][0]], axis=0)
        og = jnp.concatenate([from_left[k - 1][1], from_right[k - 1][1]], axis=0)
        part, *rest = piece(x, og, ratios[at : at + 2 * tok_rows])
        at += 2 * tok_rows
        part = part.astype(jnp.bfloat16)
        part_left.append(part[:tok_rows])
        part_right.append(part[tok_rows:])
        kept.append((x, og, *rest))
    half = tok_rows // 2
    far_part = None
    if has_far:
        part, *rest = piece(far[0], far[1], ratios[at:])
        far_part = part.astype(jnp.bfloat16)
        kept.append((far[0], far[1], *rest))

    low, high = slice(0, half), slice(half, tok_rows)

    def join(moved, part):
        return (moved.astype(jnp.float32) + part.astype(jnp.float32)).astype(jnp.bfloat16)

    def send(pair):
        return shift(pair[0], -1), shift(pair[1], 1)

    def parts_at(k, rows):
        return part_left[k - 1][rows[0]], part_right[k - 1][rows[1]]

    long_rows, short_rows = (low, high), (high, low)
    long_way = short_way = None
    if full_steps:
        short_way = send(parts_at(full_steps, short_rows))
    if has_far:
        long_way = send((far_part[low], far_part[high]))
    before = None

    def gated(parts):
        return parts if before is None else lax.optimization_barrier((parts, before))[0]

    for k in reversed(range(1, full_steps + 1)):
        if k > 1:
            sums = tuple(map(join, short_way, gated(parts_at(k - 1, short_rows))))
            short_way, before = send(sums), sums
        sums = parts_at(k, long_rows)
        if long_way is not None:
            sums = tuple(map(join, long_way, gated(sums)))
            before = sums
        long_way = send(sums)
    back_low = [long_way and long_way[0], short_way and short_way[1]]
    back_high = [long_way and long_way[1], short_way and short_way[0]]

    def closing(rows, returned):
        total = own_part[rows]
        for piece_back in returned:
            if piece_back is not None:
                total = total + piece_back.astype(jnp.float32)
        return total.astype(jnp.bfloat16)

    input_grad = jnp.concatenate([closing(low, back_low), closing(high, back_high)], axis=0)

    x_all, og_all, gg_all, ug_all, hidden_all = (
        jnp.concatenate([k[i] for k in kept], axis=0) for i in range(5)
    )

    def member_sum(product):
        total = None
        for k in reversed(range(members)):
            columns = slice(k * width, (k + 1) * width)
            block = product(columns)
            if k:
                block = member_shift(block.astype(jnp.bfloat16), k).astype(jnp.float32)
            total = block if total is None else total + block
        return total.astype(jnp.bfloat16)[None]

    gate_g = member_sum(lambda c: mm(x_all, gg_all[:, c], TN))
    up_g = member_sum(lambda c: mm(x_all, ug_all[:, c], TN))
    down_g = member_sum(lambda c: mm(hidden_all[:, c], og_all, TN))
    return (input_grad, gate_g, up_g, down_g)


def local(layer_input, output_grad, expert_ids, route_ints, w_gate, w_up, w_down):
    devices = lax.axis_size("grp") * lax.axis_size("mem")
    tok_rows, top_count = expert_ids.shape
    capacity = max(2, 9 * tok_rows * top_count // (8 * devices))
    plan = ring_plan if tok_rows <= 2 * capacity else exchange_plan
    return plan(layer_input, output_grad, expert_ids, route_ints, w_gate, w_up, w_down)


def solution(mesh):
    return jax.shard_map(
        local,
        mesh=mesh,
        in_specs=(
            P(("rep", "grp", "mem"), None),
            P(("rep", "grp", "mem"), None),
            P(("rep", "grp", "mem"), None),
            P(("rep", "grp", "mem"), None),
            P(("grp", "mem"), None, None),
            P(("grp", "mem"), None, None),
            P(("grp", "mem"), None, None),
        ),
        out_specs=(
            P(("rep", "grp", "mem"), None),
            P(("rep", "grp", "mem"), None, None),
            P(("rep", "grp", "mem"), None, None),
            P(("rep", "grp", "mem"), None, None),
        ),
        check_vma=False,
    )
```

```python
import jax
import jax.numpy as jnp
from jax import lax
from jax.sharding import PartitionSpec as P


def exchange_plan(layer_input, output_grad, expert_ids, route_ints, w_gate, w_up, w_down):
    devices = lax.axis_size("grp") * lax.axis_size("mem")
    tok_rows = layer_input.shape[0]
    model_width = layer_input.shape[1]
    top_count = expert_ids.shape[1]
    pair_count = tok_rows * top_count
    capacity = max(2, 9 * tok_rows * top_count // (8 * devices))
    slot_count = devices * capacity
    quotas = route_ints.astype(jnp.float32)
    route_ratio = quotas / jnp.sum(quotas, axis=1, keepdims=True)
    scaled = (route_ratio[:, :, None] * output_grad.astype(jnp.float32)[:, None, :]).astype(
        jnp.bfloat16
    )
    scaled = scaled.reshape(pair_count, model_width)
    flat_ids = expert_ids.reshape(pair_count)
    pair_order = jnp.arange(pair_count, dtype=jnp.int32)
    earlier = (flat_ids[None, :] == flat_ids[:, None]) & (pair_order[None, :] < pair_order[:, None])
    slot_rank = jnp.sum(earlier.astype(jnp.int32), axis=1)
    slot_key = flat_ids * capacity + slot_rank
    slot_match = slot_key[None, :] == jnp.arange(slot_count, dtype=jnp.int32)[:, None]
    filled = jnp.any(slot_match, axis=1)
    source_pair = jnp.sum(jnp.where(slot_match, pair_order[None, :], 0), axis=1)
    send_x = jnp.where(
        filled[:, None], layer_input[source_pair // top_count], jnp.zeros((), jnp.bfloat16)
    )
    send_grad = jnp.where(filled[:, None], scaled[source_pair], jnp.zeros((), jnp.bfloat16))
    recv_x, recv_grad = (
        lax.all_to_all(
            send_x.reshape(devices, capacity, model_width),
            ("grp", "mem"),
            split_axis=0,
            concat_axis=0,
            tiled=True,
        ),
        lax.all_to_all(
            send_grad.reshape(devices, capacity, model_width),
            ("grp", "mem"),
            split_axis=0,
            concat_axis=0,
            tiled=True,
        ),
    )
    rows_x = recv_x.reshape(slot_count, model_width)
    rows_grad = recv_grad.reshape(slot_count, model_width)
    gate_w = w_gate[0]
    up_w = w_up[0]
    down_w = w_down[0]
    gate_pre = jnp.dot(rows_x, gate_w, preferred_element_type=jnp.float32)
    up_pre = jnp.dot(rows_x, up_w, preferred_element_type=jnp.float32)
    sigmoid_gate = jax.nn.sigmoid(gate_pre)
    activity = gate_pre * sigmoid_gate
    hidden = (activity * up_pre).astype(jnp.bfloat16)
    hidden_grad = jnp.dot(rows_grad, down_w.T, preferred_element_type=jnp.float32)
    up_grad = (hidden_grad * activity).astype(jnp.bfloat16)
    gate_grad = (
        hidden_grad * up_pre * sigmoid_gate * (1.0 + gate_pre * (1.0 - sigmoid_gate))
    ).astype(jnp.bfloat16)
    row_grad = (
        jnp.dot(gate_grad, gate_w.T, preferred_element_type=jnp.float32)
        + jnp.dot(up_grad, up_w.T, preferred_element_type=jnp.float32)
    ).astype(jnp.bfloat16)
    returned = lax.all_to_all(
        row_grad.reshape(devices, capacity, model_width),
        ("grp", "mem"),
        split_axis=0,
        concat_axis=0,
        tiled=True,
    )
    down_wgrad = jnp.dot(hidden.T, rows_grad, preferred_element_type=jnp.float32).astype(
        jnp.bfloat16
    )
    gate_wgrad = jnp.dot(rows_x.T, gate_grad, preferred_element_type=jnp.float32).astype(
        jnp.bfloat16
    )
    up_wgrad = jnp.dot(rows_x.T, up_grad, preferred_element_type=jnp.float32).astype(jnp.bfloat16)
    back_rows = returned.reshape(slot_count, model_width)
    pair_rows = back_rows[slot_key].reshape(tok_rows, top_count, model_width)
    input_grad = jnp.sum(pair_rows.astype(jnp.float32), axis=1).astype(jnp.bfloat16)
    return (input_grad, gate_wgrad[None], up_wgrad[None], down_wgrad[None])


TN = (((0,), (0,)), ((), ()))
NT = (((1,), (1,)), ((), ()))


def ring_order(count):
    return list(range(0, count, 2)) + list(reversed(range(1, count, 2)))


def mm(a, b, dims=(((1,), (0,)), ((), ()))):
    return lax.dot_general(a, b, dims, preferred_element_type=jnp.float32)


def ring_plan(layer_input, output_grad, expert_ids, route_ints, w_gate, w_up, w_down):
    groups = lax.axis_size("grp")
    members = lax.axis_size("mem")
    tok_rows, _ = layer_input.shape
    width = w_gate.shape[2]
    span = members * width
    order = ring_order(groups)
    full_steps = (groups - 1) // 2
    has_far = groups % 2 == 0 and groups > 1

    def at_distance(k):
        return [(order[i], order[(i + k) % groups]) for i in range(groups)]

    def shift(array, k):
        return lax.ppermute(array, "grp", at_distance(k))

    def member_shift(array, step):
        return lax.ppermute(array, "mem", [(m, (m + step) % members) for m in range(members)])

    from_left, from_right = [], []
    rx, rg, lx, lg = layer_input, output_grad, layer_input, output_grad
    for _ in range(1, full_steps + 1):
        rg, lx = shift(rg, 1), shift(lx, -1)
        rx, lg = shift(rx, 1), shift(lg, -1)
        from_left.append((rx, rg))
        from_right.append((lx, lg))
    far = (shift(lx, -1), shift(rg, 1)) if has_far else None

    quotas = route_ints.astype(jnp.float32)
    route_ratio = quotas / jnp.sum(quotas, axis=1, keepdims=True)
    group_at = jnp.array(
        [[order[(order.index(g) + k) % groups] for k in range(groups)] for g in range(groups)],
        jnp.int32,
    )
    mine = jnp.arange(groups, dtype=jnp.int32)[:, None] == lax.axis_index("grp")
    chip = jnp.sum(jnp.where(mine, group_at, 0), axis=0)
    core = (lax.axis_index("mem") + jnp.arange(members, dtype=jnp.int32)) % members
    expert = chip[:, None] * members + core[None, :]
    chosen = expert_ids[None, None, :, :] == expert[:, :, None, None]
    outgoing = jnp.sum(jnp.where(chosen, route_ratio[None, None], 0.0), axis=3)

    def ratio_from(distance):
        if distance == 0:
            return outgoing[0]
        return shift(outgoing[-distance % groups], -distance)

    gates, ups, downs = [w_gate[0]], [w_up[0]], [w_down[0]]
    for k in range(1, members):
        gates.append(member_shift(w_gate[0], members - k))
        ups.append(member_shift(w_up[0], members - k))
        downs.append(member_shift(w_down[0], members - k))
    in_w = jnp.concatenate(gates + ups, axis=1)
    gate_w, up_w = in_w[:, :span], in_w[:, span:]
    down_w = jnp.concatenate(downs, axis=0)
    column = jnp.arange(span, dtype=jnp.int32)[None, :] // width

    def piece(x, og, ratio):
        r = ratio[:, 0:1]
        for m in range(1, members):
            r = jnp.where(column == m, ratio[:, m : m + 1], r)
        pre = mm(x, in_w)
        gate, up = pre[:, :span], pre[:, span:]
        s = jax.nn.sigmoid(gate)
        act = gate * s
        hidden = (act * up * r).astype(jnp.bfloat16)
        hg = r * mm(og, down_w, NT)
        ug = (hg * act).astype(jnp.bfloat16)
        gg = (hg * up * s * (1.0 + gate * (1.0 - s))).astype(jnp.bfloat16)
        part = mm(gg, gate_w, NT) + mm(ug, up_w, NT)
        return part, gg, ug, hidden

    kept = []
    own_part, *rest = piece(layer_input, output_grad, ratio_from(0).T)
    kept.append((layer_input, output_grad, *rest))
    part_left, part_right = [], []
    for k in range(1, full_steps + 1):
        x = jnp.concatenate([from_left[k - 1][0], from_right[k - 1][0]], axis=0)
        og = jnp.concatenate([from_left[k - 1][1], from_right[k - 1][1]], axis=0)
        ratio = [ratio_from(-k), ratio_from(k)]
        part, *rest = piece(x, og, jnp.concatenate(ratio, axis=1).T)
        part = part.astype(jnp.bfloat16)
        part_left.append(part[:tok_rows])
        part_right.append(part[tok_rows:])
        kept.append((x, og, *rest))
    half = tok_rows // 2
    far_part = None
    if has_far:
        part, *rest = piece(far[0], far[1], ratio_from(groups // 2).T)
        far_part = part.astype(jnp.bfloat16)
        kept.append((far[0], far[1], *rest))

    low, high = slice(0, half), slice(half, tok_rows)

    def join(moved, part):
        return (moved.astype(jnp.float32) + part.astype(jnp.float32)).astype(jnp.bfloat16)

    def send(pair):
        return shift(pair[0], -1), shift(pair[1], 1)

    def parts_at(k, rows):
        return part_left[k - 1][rows[0]], part_right[k - 1][rows[1]]

    long_rows, short_rows = (low, high), (high, low)
    long_way = short_way = None
    if full_steps:
        short_way = send(parts_at(full_steps, short_rows))
    if has_far:
        long_way = send((far_part[low], far_part[high]))
    before = None

    def gated(parts):
        return parts if before is None else lax.optimization_barrier((parts, before))[0]

    for k in reversed(range(1, full_steps + 1)):
        if k > 1:
            sums = tuple(map(join, short_way, gated(parts_at(k - 1, short_rows))))
            short_way, before = send(sums), sums
        sums = parts_at(k, long_rows)
        if long_way is not None:
            sums = tuple(map(join, long_way, gated(sums)))
            before = sums
        long_way = send(sums)
    back_low = [long_way and long_way[0], short_way and short_way[1]]
    back_high = [long_way and long_way[1], short_way and short_way[0]]

    def closing(rows, returned):
        total = own_part[rows]
        for piece_back in returned:
            if piece_back is not None:
                total = total + piece_back.astype(jnp.float32)
        return total.astype(jnp.bfloat16)

    input_grad = jnp.concatenate([closing(low, back_low), closing(high, back_high)], axis=0)

    x_all, og_all, gg_all, ug_all, hidden_all = (
        jnp.concatenate([k[i] for k in kept], axis=0) for i in range(5)
    )

    def member_sum(product):
        total = None
        for k in reversed(range(members)):
            columns = slice(k * width, (k + 1) * width)
            block = product(columns)
            if k:
                block = member_shift(block.astype(jnp.bfloat16), k).astype(jnp.float32)
            total = block if total is None else total + block
        return total.astype(jnp.bfloat16)[None]

    gate_g = member_sum(lambda c: mm(x_all, gg_all[:, c], TN))
    up_g = member_sum(lambda c: mm(x_all, ug_all[:, c], TN))
    down_g = member_sum(lambda c: mm(hidden_all[:, c], og_all, TN))
    return (input_grad, gate_g, up_g, down_g)


def local(layer_input, output_grad, expert_ids, route_ints, w_gate, w_up, w_down):
    devices = lax.axis_size("grp") * lax.axis_size("mem")
    tok_rows, top_count = expert_ids.shape
    capacity = max(2, 9 * tok_rows * top_count // (8 * devices))
    plan = ring_plan if tok_rows <= 2 * capacity else exchange_plan
    return plan(layer_input, output_grad, expert_ids, route_ints, w_gate, w_up, w_down)


def solution(mesh):
    return jax.shard_map(
        local,
        mesh=mesh,
        in_specs=(
            P(("rep", "grp", "mem"), None),
            P(("rep", "grp", "mem"), None),
            P(("rep", "grp", "mem"), None),
            P(("rep", "grp", "mem"), None),
            P(("grp", "mem"), None, None),
            P(("grp", "mem"), None, None),
            P(("grp", "mem"), None, None),
        ),
        out_specs=(
            P(("rep", "grp", "mem"), None),
            P(("rep", "grp", "mem"), None, None),
            P(("rep", "grp", "mem"), None, None),
            P(("rep", "grp", "mem"), None, None),
        ),
        check_vma=False,
    )
```

```python
import jax
import jax.numpy as jnp
from jax import lax
from jax.sharding import PartitionSpec as P


def exchange_plan(layer_input, output_grad, expert_ids, route_ints, w_gate, w_up, w_down):
    devices = lax.axis_size("grp") * lax.axis_size("mem")
    tok_rows = layer_input.shape[0]
    model_width = layer_input.shape[1]
    top_count = expert_ids.shape[1]
    pair_count = tok_rows * top_count
    capacity = max(2, 9 * tok_rows * top_count // (8 * devices))
    slot_count = devices * capacity
    quotas = route_ints.astype(jnp.float32)
    route_ratio = quotas / jnp.sum(quotas, axis=1, keepdims=True)
    scaled = (route_ratio[:, :, None] * output_grad.astype(jnp.float32)[:, None, :]).astype(
        jnp.bfloat16
    )
    scaled = scaled.reshape(pair_count, model_width)
    flat_ids = expert_ids.reshape(pair_count)
    pair_order = jnp.arange(pair_count, dtype=jnp.int32)
    earlier = (flat_ids[None, :] == flat_ids[:, None]) & (pair_order[None, :] < pair_order[:, None])
    slot_rank = jnp.sum(earlier.astype(jnp.int32), axis=1)
    slot_key = flat_ids * capacity + slot_rank
    slot_match = slot_key[None, :] == jnp.arange(slot_count, dtype=jnp.int32)[:, None]
    filled = jnp.any(slot_match, axis=1)
    source_pair = jnp.sum(jnp.where(slot_match, pair_order[None, :], 0), axis=1)
    send_x = jnp.where(
        filled[:, None], layer_input[source_pair // top_count], jnp.zeros((), jnp.bfloat16)
    )
    send_grad = jnp.where(filled[:, None], scaled[source_pair], jnp.zeros((), jnp.bfloat16))
    recv_x, recv_grad = (
        lax.all_to_all(
            send_x.reshape(devices, capacity, model_width),
            ("grp", "mem"),
            split_axis=0,
            concat_axis=0,
            tiled=True,
        ),
        lax.all_to_all(
            send_grad.reshape(devices, capacity, model_width),
            ("grp", "mem"),
            split_axis=0,
            concat_axis=0,
            tiled=True,
        ),
    )
    rows_x = recv_x.reshape(slot_count, model_width)
    rows_grad = recv_grad.reshape(slot_count, model_width)
    gate_w = w_gate[0]
    up_w = w_up[0]
    down_w = w_down[0]
    gate_pre = jnp.dot(rows_x, gate_w, preferred_element_type=jnp.float32)
    up_pre = jnp.dot(rows_x, up_w, preferred_element_type=jnp.float32)
    sigmoid_gate = jax.nn.sigmoid(gate_pre)
    activity = gate_pre * sigmoid_gate
    hidden = (activity * up_pre).astype(jnp.bfloat16)
    hidden_grad = jnp.dot(rows_grad, down_w.T, preferred_element_type=jnp.float32)
    up_grad = (hidden_grad * activity).astype(jnp.bfloat16)
    gate_grad = (
        hidden_grad * up_pre * sigmoid_gate * (1.0 + gate_pre * (1.0 - sigmoid_gate))
    ).astype(jnp.bfloat16)
    row_grad = (
        jnp.dot(gate_grad, gate_w.T, preferred_element_type=jnp.float32)
        + jnp.dot(up_grad, up_w.T, preferred_element_type=jnp.float32)
    ).astype(jnp.bfloat16)
    returned = lax.all_to_all(
        row_grad.reshape(devices, capacity, model_width),
        ("grp", "mem"),
        split_axis=0,
        concat_axis=0,
        tiled=True,
    )
    down_wgrad = jnp.dot(hidden.T, rows_grad, preferred_element_type=jnp.float32).astype(
        jnp.bfloat16
    )
    gate_wgrad = jnp.dot(rows_x.T, gate_grad, preferred_element_type=jnp.float32).astype(
        jnp.bfloat16
    )
    up_wgrad = jnp.dot(rows_x.T, up_grad, preferred_element_type=jnp.float32).astype(jnp.bfloat16)
    back_rows = returned.reshape(slot_count, model_width)
    pair_rows = back_rows[slot_key].reshape(tok_rows, top_count, model_width)
    input_grad = jnp.sum(pair_rows.astype(jnp.float32), axis=1).astype(jnp.bfloat16)
    return (input_grad, gate_wgrad[None], up_wgrad[None], down_wgrad[None])


TN = (((0,), (0,)), ((), ()))
NT = (((1,), (1,)), ((), ()))


def ring_order(count):
    return list(range(0, count, 2)) + list(reversed(range(1, count, 2)))


def mm(a, b, dims=(((1,), (0,)), ((), ()))):
    return lax.dot_general(a, b, dims, preferred_element_type=jnp.float32)


def ring_plan(layer_input, output_grad, expert_ids, route_ints, w_gate, w_up, w_down):
    groups = lax.axis_size("grp")
    members = lax.axis_size("mem")
    tok_rows, _ = layer_input.shape
    width = w_gate.shape[2]
    span = members * width
    order = ring_order(groups)
    full_steps = (groups - 1) // 2
    has_far = groups % 2 == 0 and groups > 1

    def at_distance(k):
        return [(order[i], order[(i + k) % groups]) for i in range(groups)]

    def shift(array, k):
        return lax.ppermute(array, "grp", at_distance(k))

    def member_shift(array, step):
        return lax.ppermute(array, "mem", [(m, (m + step) % members) for m in range(members)])

    from_left, from_right = [], []
    rx, rg, lx, lg = layer_input, output_grad, layer_input, output_grad
    for _ in range(1, full_steps + 1):
        rg, lx = shift(rg, 1), shift(lx, -1)
        rx, lg = shift(rx, 1), shift(lg, -1)
        from_left.append((rx, rg))
        from_right.append((lx, lg))
    far = (shift(lx, -1), shift(rg, 1)) if has_far else None

    quotas = route_ints.astype(jnp.float32)
    route_ratio = quotas / jnp.sum(quotas, axis=1, keepdims=True)
    group_at = jnp.array(
        [[order[(order.index(g) + k) % groups] for k in range(groups)] for g in range(groups)],
        jnp.int32,
    )
    mine = jnp.arange(groups, dtype=jnp.int32)[:, None] == lax.axis_index("grp")
    chip = jnp.sum(jnp.where(mine, group_at, 0), axis=0)
    core = (lax.axis_index("mem") + jnp.arange(members, dtype=jnp.int32)) % members
    expert = chip[:, None] * members + core[None, :]
    chosen = expert_ids[None, None, :, :] == expert[:, :, None, None]
    outgoing = jnp.sum(jnp.where(chosen, route_ratio[None, None], 0.0), axis=3)

    def ratio_from(distance):
        return shift(outgoing[-distance % groups], -distance)

    gates, ups, downs = [w_gate[0]], [w_up[0]], [w_down[0]]
    for k in range(1, members):
        gates.append(member_shift(w_gate[0], members - k))
        ups.append(member_shift(w_up[0], members - k))
        downs.append(member_shift(w_down[0], members - k))
    gate_w = jnp.concatenate(gates, axis=1)
    up_w = jnp.concatenate(ups, axis=1)
    down_w = jnp.concatenate(downs, axis=0)
    column = jnp.arange(span, dtype=jnp.int32)[None, :] // width

    def piece(x, og, ratio):
        r = ratio[:, 0:1]
        for m in range(1, members):
            r = jnp.where(column == m, ratio[:, m : m + 1], r)
        gate, up = mm(x, gate_w), mm(x, up_w)
        s = jax.nn.sigmoid(gate)
        act = gate * s
        hidden = (act * up * r).astype(jnp.bfloat16)
        hg = r * mm(og, down_w, NT)
        ug = (hg * act).astype(jnp.bfloat16)
        gg = (hg * up * s * (1.0 + gate * (1.0 - s))).astype(jnp.bfloat16)
        part = mm(gg, gate_w, NT) + mm(ug, up_w, NT)
        return part, gg, ug, hidden

    kept, part_left, part_right = [], [], []

    def step_piece(steps, ratios):
        x = jnp.concatenate([x for x, _ in steps], axis=0)
        og = jnp.concatenate([og for _, og in steps], axis=0)
        ratio = jnp.concatenate(ratios, axis=1).T
        if kept:
            ratio = lax.optimization_barrier((ratio, kept[-1][2]))[0]
        part, *rest = piece(x, og, ratio)
        kept.append((x, og, *rest))
        part = part.astype(jnp.bfloat16)
        return part[:tok_rows], part[tok_rows:]

    for k in range(1, full_steps + 1):
        ratio = [ratio_from(-k), ratio_from(k)]
        parts = step_piece((from_left[k - 1], from_right[k - 1]), ratio)
        part_left.append(parts[0])
        part_right.append(parts[1])
    half = tok_rows // 2
    steps, ratio = [(layer_input, output_grad)], [outgoing[0]]
    if has_far:
        steps.append(far)
        ratio.append(ratio_from(groups // 2))
    own_part, far_part = step_piece(steps, ratio)

    low, high = slice(0, half), slice(half, tok_rows)

    def join(moved, part):
        return (moved.astype(jnp.float32) + part.astype(jnp.float32)).astype(jnp.bfloat16)

    def send(pair):
        return shift(pair[0], -1), shift(pair[1], 1)

    def parts_at(k, rows):
        return part_left[k - 1][rows[0]], part_right[k - 1][rows[1]]

    long_rows, short_rows = (low, high), (high, low)
    long_way = short_way = None
    if full_steps:
        short_way = send(parts_at(full_steps, short_rows))
    if has_far:
        long_way = send((far_part[low], far_part[high]))
    before = None

    def gated(parts):
        return parts if before is None else lax.optimization_barrier((parts, before))[0]

    for k in reversed(range(1, full_steps + 1)):
        if k > 1:
            sums = tuple(map(join, short_way, gated(parts_at(k - 1, short_rows))))
            short_way, before = send(sums), sums
        sums = parts_at(k, long_rows)
        if long_way is not None:
            sums = tuple(map(join, long_way, gated(sums)))
            before = sums
        long_way = send(sums)
    back_low = [long_way and long_way[0], short_way and short_way[1]]
    back_high = [long_way and long_way[1], short_way and short_way[0]]

    def closing(rows, returned):
        total = own_part[rows].astype(jnp.float32)
        for piece_back in returned:
            if piece_back is not None:
                total = total + piece_back.astype(jnp.float32)
        return total.astype(jnp.bfloat16)

    input_grad = jnp.concatenate([closing(low, back_low), closing(high, back_high)], axis=0)

    x_all, og_all, gg_all, ug_all, hidden_all = (
        jnp.concatenate([k[i] for k in kept], axis=0) for i in range(5)
    )

    def member_sum(product):
        total = None
        for k in reversed(range(members)):
            columns = slice(k * width, (k + 1) * width)
            block = product(columns)
            if k:
                block = member_shift(block.astype(jnp.bfloat16), k).astype(jnp.float32)
            total = block if total is None else total + block
        return total.astype(jnp.bfloat16)[None]

    gate_g = member_sum(lambda c: mm(x_all, gg_all[:, c], TN))
    up_g = member_sum(lambda c: mm(x_all, ug_all[:, c], TN))
    down_g = member_sum(lambda c: mm(hidden_all[:, c], og_all, TN))
    return (input_grad, gate_g, up_g, down_g)


def local(layer_input, output_grad, expert_ids, route_ints, w_gate, w_up, w_down):
    devices = lax.axis_size("grp") * lax.axis_size("mem")
    tok_rows, top_count = expert_ids.shape
    capacity = max(2, 9 * tok_rows * top_count // (8 * devices))
    plan = ring_plan if tok_rows <= 2 * capacity else exchange_plan
    return plan(layer_input, output_grad, expert_ids, route_ints, w_gate, w_up, w_down)


def solution(mesh):
    return jax.shard_map(
        local,
        mesh=mesh,
        in_specs=(
            P(("rep", "grp", "mem"), None),
            P(("rep", "grp", "mem"), None),
            P(("rep", "grp", "mem"), None),
            P(("rep", "grp", "mem"), None),
            P(("grp", "mem"), None, None),
            P(("grp", "mem"), None, None),
            P(("grp", "mem"), None, None),
        ),
        out_specs=(
            P(("rep", "grp", "mem"), None),
            P(("rep", "grp", "mem"), None, None),
            P(("rep", "grp", "mem"), None, None),
            P(("rep", "grp", "mem"), None, None),
        ),
        check_vma=False,
    )
```

```python
import jax
import jax.numpy as jnp
from jax import lax
from jax.sharding import PartitionSpec as P


def exchange_plan(layer_input, output_grad, expert_ids, route_ints, w_gate, w_up, w_down):
    devices = lax.axis_size("grp") * lax.axis_size("mem")
    tok_rows = layer_input.shape[0]
    model_width = layer_input.shape[1]
    top_count = expert_ids.shape[1]
    pair_count = tok_rows * top_count
    capacity = max(2, 9 * tok_rows * top_count // (8 * devices))
    slot_count = devices * capacity
    quotas = route_ints.astype(jnp.float32)
    route_ratio = quotas / jnp.sum(quotas, axis=1, keepdims=True)
    scaled = (route_ratio[:, :, None] * output_grad.astype(jnp.float32)[:, None, :]).astype(
        jnp.bfloat16
    )
    scaled = scaled.reshape(pair_count, model_width)
    flat_ids = expert_ids.reshape(pair_count)
    pair_order = jnp.arange(pair_count, dtype=jnp.int32)
    earlier = (flat_ids[None, :] == flat_ids[:, None]) & (pair_order[None, :] < pair_order[:, None])
    slot_rank = jnp.sum(earlier.astype(jnp.int32), axis=1)
    slot_key = flat_ids * capacity + slot_rank
    slot_match = slot_key[None, :] == jnp.arange(slot_count, dtype=jnp.int32)[:, None]
    filled = jnp.any(slot_match, axis=1)
    source_pair = jnp.sum(jnp.where(slot_match, pair_order[None, :], 0), axis=1)
    send_x = jnp.where(
        filled[:, None], layer_input[source_pair // top_count], jnp.zeros((), jnp.bfloat16)
    )
    send_grad = jnp.where(filled[:, None], scaled[source_pair], jnp.zeros((), jnp.bfloat16))
    recv_x, recv_grad = (
        lax.all_to_all(
            send_x.reshape(devices, capacity, model_width),
            ("grp", "mem"),
            split_axis=0,
            concat_axis=0,
            tiled=True,
        ),
        lax.all_to_all(
            send_grad.reshape(devices, capacity, model_width),
            ("grp", "mem"),
            split_axis=0,
            concat_axis=0,
            tiled=True,
        ),
    )
    rows_x = recv_x.reshape(slot_count, model_width)
    rows_grad = recv_grad.reshape(slot_count, model_width)
    gate_w = w_gate[0]
    up_w = w_up[0]
    down_w = w_down[0]
    gate_pre = jnp.dot(rows_x, gate_w, preferred_element_type=jnp.float32)
    up_pre = jnp.dot(rows_x, up_w, preferred_element_type=jnp.float32)
    sigmoid_gate = jax.nn.sigmoid(gate_pre)
    activity = gate_pre * sigmoid_gate
    hidden = (activity * up_pre).astype(jnp.bfloat16)
    hidden_grad = jnp.dot(rows_grad, down_w.T, preferred_element_type=jnp.float32)
    up_grad = (hidden_grad * activity).astype(jnp.bfloat16)
    gate_grad = (
        hidden_grad * up_pre * sigmoid_gate * (1.0 + gate_pre * (1.0 - sigmoid_gate))
    ).astype(jnp.bfloat16)
    row_grad = (
        jnp.dot(gate_grad, gate_w.T, preferred_element_type=jnp.float32)
        + jnp.dot(up_grad, up_w.T, preferred_element_type=jnp.float32)
    ).astype(jnp.bfloat16)
    returned = lax.all_to_all(
        row_grad.reshape(devices, capacity, model_width),
        ("grp", "mem"),
        split_axis=0,
        concat_axis=0,
        tiled=True,
    )
    down_wgrad = jnp.dot(hidden.T, rows_grad, preferred_element_type=jnp.float32).astype(
        jnp.bfloat16
    )
    gate_wgrad = jnp.dot(rows_x.T, gate_grad, preferred_element_type=jnp.float32).astype(
        jnp.bfloat16
    )
    up_wgrad = jnp.dot(rows_x.T, up_grad, preferred_element_type=jnp.float32).astype(jnp.bfloat16)
    back_rows = returned.reshape(slot_count, model_width)
    pair_rows = back_rows[slot_key].reshape(tok_rows, top_count, model_width)
    input_grad = jnp.sum(pair_rows.astype(jnp.float32), axis=1).astype(jnp.bfloat16)
    return (input_grad, gate_wgrad[None], up_wgrad[None], down_wgrad[None])


TN = (((0,), (0,)), ((), ()))
NT = (((1,), (1,)), ((), ()))


def ring_order(count):
    return list(range(0, count, 2)) + list(reversed(range(1, count, 2)))


def mm(a, b, dims=(((1,), (0,)), ((), ()))):
    return lax.dot_general(a, b, dims, preferred_element_type=jnp.float32)


def ring_plan(layer_input, output_grad, expert_ids, route_ints, w_gate, w_up, w_down):
    groups = lax.axis_size("grp")
    members = lax.axis_size("mem")
    tok_rows, _ = layer_input.shape
    width = w_gate.shape[2]
    span = members * width
    order = ring_order(groups)
    full_steps = (groups - 1) // 2
    has_far = groups % 2 == 0 and groups > 1

    def at_distance(k):
        return [(order[i], order[(i + k) % groups]) for i in range(groups)]

    def shift(array, k):
        return lax.ppermute(array, "grp", at_distance(k))

    def member_shift(array, step):
        return lax.ppermute(array, "mem", [(m, (m + step) % members) for m in range(members)])

    from_left, from_right = [], []
    rx, rg, lx, lg = layer_input, output_grad, layer_input, output_grad
    for _ in range(1, full_steps + 1):
        rg, lx = shift(rg, 1), shift(lx, -1)
        rx, lg = shift(rx, 1), shift(lg, -1)
        from_left.append((rx, rg))
        from_right.append((lx, lg))
    far = (shift(lx, -1), shift(rg, 1)) if has_far else None

    quotas = route_ints.astype(jnp.float32)
    route_ratio = quotas / jnp.sum(quotas, axis=1, keepdims=True)
    group_at = jnp.array(
        [[order[(order.index(g) + k) % groups] for k in range(groups)] for g in range(groups)],
        jnp.int32,
    )
    mine = jnp.arange(groups, dtype=jnp.int32)[:, None] == lax.axis_index("grp")
    chip = jnp.sum(jnp.where(mine, group_at, 0), axis=0)
    core = (lax.axis_index("mem") + jnp.arange(members, dtype=jnp.int32)) % members
    expert = chip[:, None] * members + core[None, :]
    chosen = expert_ids[None, None, :, :] == expert[:, :, None, None]
    outgoing = jnp.sum(jnp.where(chosen, route_ratio[None, None], 0.0), axis=3)

    blocks = [outgoing[d] for d in range(groups)]
    for bit in range((groups - 1).bit_length()):
        going = [d for d in range(groups) if d >> bit & 1]
        packed = jnp.concatenate([blocks[d] for d in going], axis=0)
        moved = shift(packed, 1 << bit)
        for i, d in enumerate(going):
            blocks[d] = moved[i * members : (i + 1) * members]

    def ratio_from(distance):
        return blocks[-distance % groups]

    gates, ups, downs = [w_gate[0]], [w_up[0]], [w_down[0]]
    for k in range(1, members):
        gates.append(member_shift(w_gate[0], members - k))
        ups.append(member_shift(w_up[0], members - k))
        downs.append(member_shift(w_down[0], members - k))
    gate_w = jnp.concatenate(gates, axis=1)
    up_w = jnp.concatenate(ups, axis=1)
    down_w = jnp.concatenate(downs, axis=0)
    column = jnp.arange(span, dtype=jnp.int32)[None, :] // width

    def piece(x, og, ratio):
        r = ratio[:, 0:1]
        for m in range(1, members):
            r = jnp.where(column == m, ratio[:, m : m + 1], r)
        gate, up = mm(x, gate_w), mm(x, up_w)
        s = jax.nn.sigmoid(gate)
        act = gate * s
        hidden = (act * up * r).astype(jnp.bfloat16)
        hg = r * mm(og, down_w, NT)
        ug = (hg * act).astype(jnp.bfloat16)
        gg = (hg * up * s * (1.0 + gate * (1.0 - s))).astype(jnp.bfloat16)
        part = mm(gg, gate_w, NT) + mm(ug, up_w, NT)
        return part, gg, ug, hidden

    kept, part_left, part_right = [], [], []

    def step_piece(steps, ratios):
        x = jnp.concatenate([x for x, _ in steps], axis=0)
        og = jnp.concatenate([og for _, og in steps], axis=0)
        ratio = jnp.concatenate(ratios, axis=1).T
        if kept:
            ratio = lax.optimization_barrier((ratio, kept[-1][2]))[0]
        part, *rest = piece(x, og, ratio)
        kept.append((x, og, *rest))
        part = part.astype(jnp.bfloat16)
        return part[:tok_rows], part[tok_rows:]

    for k in range(1, full_steps + 1):
        ratio = [ratio_from(-k), ratio_from(k)]
        parts = step_piece((from_left[k - 1], from_right[k - 1]), ratio)
        part_left.append(parts[0])
        part_right.append(parts[1])
    half = tok_rows // 2
    steps, ratio = [(layer_input, output_grad)], [outgoing[0]]
    if has_far:
        steps.append(far)
        ratio.append(ratio_from(groups // 2))
    own_part, far_part = step_piece(steps, ratio)

    low, high = slice(0, half), slice(half, tok_rows)

    def join(moved, part):
        return (moved.astype(jnp.float32) + part.astype(jnp.float32)).astype(jnp.bfloat16)

    def send(pair):
        return shift(pair[0], -1), shift(pair[1], 1)

    def parts_at(k, rows):
        return part_left[k - 1][rows[0]], part_right[k - 1][rows[1]]

    long_rows, short_rows = (low, high), (high, low)
    long_way = short_way = None
    if full_steps:
        short_way = send(parts_at(full_steps, short_rows))
    if has_far:
        long_way = send((far_part[low], far_part[high]))
    before = None

    def gated(parts):
        return parts if before is None else lax.optimization_barrier((parts, before))[0]

    for k in reversed(range(1, full_steps + 1)):
        if k > 1:
            sums = tuple(map(join, short_way, gated(parts_at(k - 1, short_rows))))
            short_way, before = send(sums), sums
        sums = parts_at(k, long_rows)
        if long_way is not None:
            sums = tuple(map(join, long_way, gated(sums)))
            before = sums
        long_way = send(sums)
    back_low = [long_way and long_way[0], short_way and short_way[1]]
    back_high = [long_way and long_way[1], short_way and short_way[0]]

    def closing(rows, returned):
        total = own_part[rows].astype(jnp.float32)
        for piece_back in returned:
            if piece_back is not None:
                total = total + piece_back.astype(jnp.float32)
        return total.astype(jnp.bfloat16)

    input_grad = jnp.concatenate([closing(low, back_low), closing(high, back_high)], axis=0)

    x_all, og_all, gg_all, ug_all, hidden_all = (
        jnp.concatenate([k[i] for k in kept], axis=0) for i in range(5)
    )

    def member_sum(product):
        total = None
        for k in reversed(range(members)):
            columns = slice(k * width, (k + 1) * width)
            block = product(columns)
            if k:
                block = member_shift(block.astype(jnp.bfloat16), k).astype(jnp.float32)
            total = block if total is None else total + block
        return total.astype(jnp.bfloat16)[None]

    gate_g = member_sum(lambda c: mm(x_all, gg_all[:, c], TN))
    up_g = member_sum(lambda c: mm(x_all, ug_all[:, c], TN))
    down_g = member_sum(lambda c: mm(hidden_all[:, c], og_all, TN))
    return (input_grad, gate_g, up_g, down_g)


def local(layer_input, output_grad, expert_ids, route_ints, w_gate, w_up, w_down):
    devices = lax.axis_size("grp") * lax.axis_size("mem")
    tok_rows, top_count = expert_ids.shape
    capacity = max(2, 9 * tok_rows * top_count // (8 * devices))
    plan = ring_plan if tok_rows <= 2 * capacity else exchange_plan
    return plan(layer_input, output_grad, expert_ids, route_ints, w_gate, w_up, w_down)


def solution(mesh):
    return jax.shard_map(
        local,
        mesh=mesh,
        in_specs=(
            P(("rep", "grp", "mem"), None),
            P(("rep", "grp", "mem"), None),
            P(("rep", "grp", "mem"), None),
            P(("rep", "grp", "mem"), None),
            P(("grp", "mem"), None, None),
            P(("grp", "mem"), None, None),
            P(("grp", "mem"), None, None),
        ),
        out_specs=(
            P(("rep", "grp", "mem"), None),
            P(("rep", "grp", "mem"), None, None),
            P(("rep", "grp", "mem"), None, None),
            P(("rep", "grp", "mem"), None, None),
        ),
        check_vma=False,
    )
```

```python
import jax
import jax.numpy as jnp
from jax import lax
from jax.sharding import PartitionSpec as P


def exchange_plan(layer_input, output_grad, expert_ids, route_ints, w_gate, w_up, w_down):
    devices = lax.axis_size("grp") * lax.axis_size("mem")
    tok_rows = layer_input.shape[0]
    model_width = layer_input.shape[1]
    top_count = expert_ids.shape[1]
    pair_count = tok_rows * top_count
    capacity = max(2, 9 * tok_rows * top_count // (8 * devices))
    slot_count = devices * capacity
    quotas = route_ints.astype(jnp.float32)
    route_ratio = quotas / jnp.sum(quotas, axis=1, keepdims=True)
    scaled = (route_ratio[:, :, None] * output_grad.astype(jnp.float32)[:, None, :]).astype(
        jnp.bfloat16
    )
    scaled = scaled.reshape(pair_count, model_width)
    flat_ids = expert_ids.reshape(pair_count)
    pair_order = jnp.arange(pair_count, dtype=jnp.int32)
    earlier = (flat_ids[None, :] == flat_ids[:, None]) & (pair_order[None, :] < pair_order[:, None])
    slot_rank = jnp.sum(earlier.astype(jnp.int32), axis=1)
    slot_key = flat_ids * capacity + slot_rank
    slot_match = slot_key[None, :] == jnp.arange(slot_count, dtype=jnp.int32)[:, None]
    filled = jnp.any(slot_match, axis=1)
    source_pair = jnp.sum(jnp.where(slot_match, pair_order[None, :], 0), axis=1)
    send_x = jnp.where(
        filled[:, None], layer_input[source_pair // top_count], jnp.zeros((), jnp.bfloat16)
    )
    send_grad = jnp.where(filled[:, None], scaled[source_pair], jnp.zeros((), jnp.bfloat16))
    recv_x, recv_grad = (
        lax.all_to_all(
            send_x.reshape(devices, capacity, model_width),
            ("grp", "mem"),
            split_axis=0,
            concat_axis=0,
            tiled=True,
        ),
        lax.all_to_all(
            send_grad.reshape(devices, capacity, model_width),
            ("grp", "mem"),
            split_axis=0,
            concat_axis=0,
            tiled=True,
        ),
    )
    rows_x = recv_x.reshape(slot_count, model_width)
    rows_grad = recv_grad.reshape(slot_count, model_width)
    gate_w = w_gate[0]
    up_w = w_up[0]
    down_w = w_down[0]
    gate_pre = jnp.dot(rows_x, gate_w, preferred_element_type=jnp.float32)
    up_pre = jnp.dot(rows_x, up_w, preferred_element_type=jnp.float32)
    sigmoid_gate = jax.nn.sigmoid(gate_pre)
    activity = gate_pre * sigmoid_gate
    hidden = (activity * up_pre).astype(jnp.bfloat16)
    hidden_grad = jnp.dot(rows_grad, down_w.T, preferred_element_type=jnp.float32)
    up_grad = (hidden_grad * activity).astype(jnp.bfloat16)
    gate_grad = (
        hidden_grad * up_pre * sigmoid_gate * (1.0 + gate_pre * (1.0 - sigmoid_gate))
    ).astype(jnp.bfloat16)
    row_grad = (
        jnp.dot(gate_grad, gate_w.T, preferred_element_type=jnp.float32)
        + jnp.dot(up_grad, up_w.T, preferred_element_type=jnp.float32)
    ).astype(jnp.bfloat16)
    returned = lax.all_to_all(
        row_grad.reshape(devices, capacity, model_width),
        ("grp", "mem"),
        split_axis=0,
        concat_axis=0,
        tiled=True,
    )
    down_wgrad = jnp.dot(hidden.T, rows_grad, preferred_element_type=jnp.float32).astype(
        jnp.bfloat16
    )
    gate_wgrad = jnp.dot(rows_x.T, gate_grad, preferred_element_type=jnp.float32).astype(
        jnp.bfloat16
    )
    up_wgrad = jnp.dot(rows_x.T, up_grad, preferred_element_type=jnp.float32).astype(jnp.bfloat16)
    back_rows = returned.reshape(slot_count, model_width)
    pair_rows = back_rows[slot_key].reshape(tok_rows, top_count, model_width)
    input_grad = jnp.sum(pair_rows.astype(jnp.float32), axis=1).astype(jnp.bfloat16)
    return (input_grad, gate_wgrad[None], up_wgrad[None], down_wgrad[None])


TN = (((0,), (0,)), ((), ()))
NT = (((1,), (1,)), ((), ()))


def ring_order(count):
    return list(range(0, count, 2)) + list(reversed(range(1, count, 2)))


def mm(a, b, dims=(((1,), (0,)), ((), ()))):
    return lax.dot_general(a, b, dims, preferred_element_type=jnp.float32)


def ring_plan(layer_input, output_grad, expert_ids, route_ints, w_gate, w_up, w_down):
    groups = lax.axis_size("grp")
    members = lax.axis_size("mem")
    tok_rows, _ = layer_input.shape
    width = w_gate.shape[2]
    span = members * width
    order = ring_order(groups)
    full_steps = (groups - 1) // 2
    has_far = groups % 2 == 0 and groups > 1

    def at_distance(k):
        return [(order[i], order[(i + k) % groups]) for i in range(groups)]

    def shift(array, k):
        return lax.ppermute(array, "grp", at_distance(k))

    def member_shift(array, step):
        return lax.ppermute(array, "mem", [(m, (m + step) % members) for m in range(members)])

    half = tok_rows // 2
    low, high = slice(0, half), slice(half, tok_rows)
    rg, lx = output_grad, layer_input
    rx = {high: layer_input[high], low: layer_input[low]}
    lg = {low: output_grad[low], high: output_grad[high]}
    from_left, from_right = [], []
    for k in range(1, full_steps + 1):
        rg, lx = shift(rg, 1), shift(lx, -1)
        rx = {high: shift(rx[high], 1), low: shift(rx[low], 1)}
        lg = {low: shift(lg[low], -1), high: shift(lg[high], -1)}
        from_left.append((rx, {low: rg[low], high: rg[high]}))
        from_right.append(({low: lx[low], high: lx[high]}, lg, lx))
        from_left[-1] += (rg,)
    far = (shift(lx, -1), shift(rg, 1)) if has_far else None

    quotas = route_ints.astype(jnp.float32)
    route_ratio = quotas / jnp.sum(quotas, axis=1, keepdims=True)
    group_at = jnp.array(
        [[order[(order.index(g) + k) % groups] for k in range(groups)] for g in range(groups)],
        jnp.int32,
    )
    mine = jnp.arange(groups, dtype=jnp.int32)[:, None] == lax.axis_index("grp")
    chip = jnp.sum(jnp.where(mine, group_at, 0), axis=0)
    core = (lax.axis_index("mem") + jnp.arange(members, dtype=jnp.int32)) % members
    expert = chip[:, None] * members + core[None, :]
    chosen = expert_ids[None, None, :, :] == expert[:, :, None, None]
    outgoing = jnp.sum(jnp.where(chosen, route_ratio[None, None], 0.0), axis=3)

    blocks = [outgoing[d] for d in range(groups)]
    for bit in range((groups - 1).bit_length()):
        going = [d for d in range(groups) if d >> bit & 1]
        packed = jnp.concatenate([blocks[d] for d in going], axis=0)
        moved = shift(packed, 1 << bit)
        for i, d in enumerate(going):
            blocks[d] = moved[i * members : (i + 1) * members]

    def ratio_from(distance):
        return blocks[-distance % groups]

    gates, ups, downs = [w_gate[0]], [w_up[0]], [w_down[0]]
    for k in range(1, members):
        gates.append(member_shift(w_gate[0], members - k))
        ups.append(member_shift(w_up[0], members - k))
        downs.append(member_shift(w_down[0], members - k))
    gate_w = jnp.concatenate(gates, axis=1)
    up_w = jnp.concatenate(ups, axis=1)
    down_w = jnp.concatenate(downs, axis=0)
    column = jnp.arange(span, dtype=jnp.int32)[None, :] // width

    def piece(x, og, ratio):
        r = ratio[:, 0:1]
        for m in range(1, members):
            r = jnp.where(column == m, ratio[:, m : m + 1], r)
        gate, up = mm(x, gate_w), mm(x, up_w)
        s = jax.nn.sigmoid(gate)
        act = gate * s
        hidden = (act * up * r).astype(jnp.bfloat16)
        hg = r * mm(og, down_w, NT)
        ug = (hg * act).astype(jnp.bfloat16)
        gg = (hg * up * s * (1.0 + gate * (1.0 - s))).astype(jnp.bfloat16)
        part = mm(gg, gate_w, NT) + mm(ug, up_w, NT)
        return part, gg, ug, hidden

    kept = []

    def step_piece(xs, ogs, ratios, apart=False):
        x, og = jnp.concatenate(xs, axis=0), jnp.concatenate(ogs, axis=0)
        if apart:
            x, og = lax.optimization_barrier((x, og))
        ratio = jnp.concatenate(ratios, axis=1).T
        if kept:
            ratio = lax.optimization_barrier((ratio, kept[-1][2]))[0]
        part, *rest = piece(x, og, ratio)
        kept.append((x, og, *rest))
        return part.astype(jnp.bfloat16)

    parts = {}
    for k in range(1, full_steps):
        lefts, rights = from_left[k - 1], from_right[k - 1]
        xs = [lefts[0][low], lefts[0][high], rights[2]]
        ogs = [lefts[2], rights[1][low], rights[1][high]]
        part = step_piece(xs, ogs, [ratio_from(-k), ratio_from(k)])
        parts[k] = [
            {rows: part[at + rows.start : at + rows.stop] for rows in (low, high)}
            for at in (0, tok_rows)
        ]
    own_and_far = [(layer_input, output_grad)] + [far] * has_far
    ratio = [outgoing[0]] + [ratio_from(groups // 2)] * has_far
    part = step_piece([x for x, _ in own_and_far], [og for _, og in own_and_far], ratio)
    own_part, far_part = part[:tok_rows], part[tok_rows:]
    if full_steps:
        k = full_steps
        lefts, rights = from_left[k - 1], from_right[k - 1]
        parts[k] = [{}, {}]
        for one, two in ((high, low), (low, high)):
            part = step_piece(
                [lefts[0][one], rights[0][two]],
                [lefts[1][one], rights[1][two]],
                [ratio_from(-k)[:, one], ratio_from(k)[:, two]],
                apart=True,
            )
            parts[k][0][one], parts[k][1][two] = part[:half], part[half:]

    def join(moved, part):
        return (moved.astype(jnp.float32) + part.astype(jnp.float32)).astype(jnp.bfloat16)

    def send(pair):
        return shift(pair[0], -1), shift(pair[1], 1)

    def parts_at(k, rows):
        return parts[k][0][rows[0]], parts[k][1][rows[1]]

    long_rows, short_rows = (low, high), (high, low)
    long_way = short_way = before = None

    def gated(pair):
        return pair if before is None else lax.optimization_barrier((pair, before))[0]

    if has_far:
        long_way = send((far_part[low], far_part[high]))
    for k in reversed(range(1, full_steps + 1)):
        sums = parts_at(k, short_rows)
        if short_way is not None:
            sums = before = tuple(map(join, short_way, gated(sums)))
        short_way = send(sums)
        sums = parts_at(k, long_rows)
        if long_way is not None:
            sums = before = tuple(map(join, long_way, gated(sums)))
        long_way = send(sums)
    back_low = [long_way and long_way[0], short_way and short_way[1]]
    back_high = [long_way and long_way[1], short_way and short_way[0]]

    def closing(rows, returned):
        total = own_part[rows].astype(jnp.float32)
        for piece_back in returned:
            if piece_back is not None:
                total = total + piece_back.astype(jnp.float32)
        return total.astype(jnp.bfloat16)

    input_grad = jnp.concatenate([closing(low, back_low), closing(high, back_high)], axis=0)

    x_all, og_all, gg_all, ug_all, hidden_all = (
        jnp.concatenate([k[i] for k in kept], axis=0) for i in range(5)
    )

    def member_sum(product, axis):
        both = lax.optimization_barrier(product.astype(jnp.bfloat16))
        blocks = jnp.split(both, members, axis=axis)
        moved = [member_shift(blocks[k], k) for k in range(1, members)]
        total = sum(block.astype(jnp.float32) for block in [blocks[0], *moved])
        return total.astype(jnp.bfloat16)[None]

    gate_p = mm(x_all, gg_all, TN)
    up_p = mm(x_all, ug_all, TN)
    down_p = mm(hidden_all, og_all, TN)
    gate_g = member_sum(gate_p, 1)
    up_g = member_sum(up_p, 1)
    down_g = member_sum(down_p, 0)
    return (input_grad, gate_g, up_g, down_g)


def local(layer_input, output_grad, expert_ids, route_ints, w_gate, w_up, w_down):
    devices = lax.axis_size("grp") * lax.axis_size("mem")
    tok_rows, top_count = expert_ids.shape
    capacity = max(2, 9 * tok_rows * top_count // (8 * devices))
    plan = ring_plan if tok_rows <= 2 * capacity else exchange_plan
    return plan(layer_input, output_grad, expert_ids, route_ints, w_gate, w_up, w_down)


def solution(mesh):
    return jax.shard_map(
        local,
        mesh=mesh,
        in_specs=(
            P(("rep", "grp", "mem"), None),
            P(("rep", "grp", "mem"), None),
            P(("rep", "grp", "mem"), None),
            P(("rep", "grp", "mem"), None),
            P(("grp", "mem"), None, None),
            P(("grp", "mem"), None, None),
            P(("grp", "mem"), None, None),
        ),
        out_specs=(
            P(("rep", "grp", "mem"), None),
            P(("rep", "grp", "mem"), None, None),
            P(("rep", "grp", "mem"), None, None),
            P(("rep", "grp", "mem"), None, None),
        ),
        check_vma=False,
    )
```

```python
import jax
import jax.numpy as jnp
from jax import lax
from jax.sharding import PartitionSpec as P


def exchange_plan(layer_input, output_grad, expert_ids, route_ints, w_gate, w_up, w_down):
    devices = lax.axis_size("grp") * lax.axis_size("mem")
    tok_rows = layer_input.shape[0]
    model_width = layer_input.shape[1]
    top_count = expert_ids.shape[1]
    pair_count = tok_rows * top_count
    capacity = max(2, 9 * tok_rows * top_count // (8 * devices))
    slot_count = devices * capacity
    quotas = route_ints.astype(jnp.float32)
    route_ratio = quotas / jnp.sum(quotas, axis=1, keepdims=True)
    scaled = (route_ratio[:, :, None] * output_grad.astype(jnp.float32)[:, None, :]).astype(
        jnp.bfloat16
    )
    scaled = scaled.reshape(pair_count, model_width)
    flat_ids = expert_ids.reshape(pair_count)
    pair_order = jnp.arange(pair_count, dtype=jnp.int32)
    earlier = (flat_ids[None, :] == flat_ids[:, None]) & (pair_order[None, :] < pair_order[:, None])
    slot_rank = jnp.sum(earlier.astype(jnp.int32), axis=1)
    slot_key = flat_ids * capacity + slot_rank
    slot_match = slot_key[None, :] == jnp.arange(slot_count, dtype=jnp.int32)[:, None]
    filled = jnp.any(slot_match, axis=1)
    source_pair = jnp.sum(jnp.where(slot_match, pair_order[None, :], 0), axis=1)
    send_x = jnp.where(
        filled[:, None], layer_input[source_pair // top_count], jnp.zeros((), jnp.bfloat16)
    )
    send_grad = jnp.where(filled[:, None], scaled[source_pair], jnp.zeros((), jnp.bfloat16))
    recv_x, recv_grad = (
        lax.all_to_all(
            send_x.reshape(devices, capacity, model_width),
            ("grp", "mem"),
            split_axis=0,
            concat_axis=0,
            tiled=True,
        ),
        lax.all_to_all(
            send_grad.reshape(devices, capacity, model_width),
            ("grp", "mem"),
            split_axis=0,
            concat_axis=0,
            tiled=True,
        ),
    )
    rows_x = recv_x.reshape(slot_count, model_width)
    rows_grad = recv_grad.reshape(slot_count, model_width)
    gate_w = w_gate[0]
    up_w = w_up[0]
    down_w = w_down[0]
    gate_pre = jnp.dot(rows_x, gate_w, preferred_element_type=jnp.float32)
    up_pre = jnp.dot(rows_x, up_w, preferred_element_type=jnp.float32)
    sigmoid_gate = jax.nn.sigmoid(gate_pre)
    activity = gate_pre * sigmoid_gate
    hidden = (activity * up_pre).astype(jnp.bfloat16)
    hidden_grad = jnp.dot(rows_grad, down_w.T, preferred_element_type=jnp.float32)
    up_grad = (hidden_grad * activity).astype(jnp.bfloat16)
    gate_grad = (
        hidden_grad * up_pre * sigmoid_gate * (1.0 + gate_pre * (1.0 - sigmoid_gate))
    ).astype(jnp.bfloat16)
    row_grad = (
        jnp.dot(gate_grad, gate_w.T, preferred_element_type=jnp.float32)
        + jnp.dot(up_grad, up_w.T, preferred_element_type=jnp.float32)
    ).astype(jnp.bfloat16)
    returned = lax.all_to_all(
        row_grad.reshape(devices, capacity, model_width),
        ("grp", "mem"),
        split_axis=0,
        concat_axis=0,
        tiled=True,
    )
    down_wgrad = jnp.dot(hidden.T, rows_grad, preferred_element_type=jnp.float32).astype(
        jnp.bfloat16
    )
    gate_wgrad = jnp.dot(rows_x.T, gate_grad, preferred_element_type=jnp.float32).astype(
        jnp.bfloat16
    )
    up_wgrad = jnp.dot(rows_x.T, up_grad, preferred_element_type=jnp.float32).astype(jnp.bfloat16)
    back_rows = returned.reshape(slot_count, model_width)
    pair_rows = back_rows[slot_key].reshape(tok_rows, top_count, model_width)
    input_grad = jnp.sum(pair_rows.astype(jnp.float32), axis=1).astype(jnp.bfloat16)
    return (input_grad, gate_wgrad[None], up_wgrad[None], down_wgrad[None])


TN = (((0,), (0,)), ((), ()))
NT = (((1,), (1,)), ((), ()))


def ring_order(count):
    return list(range(0, count, 2)) + list(reversed(range(1, count, 2)))


def mm(a, b, dims=(((1,), (0,)), ((), ()))):
    return lax.dot_general(a, b, dims, preferred_element_type=jnp.float32)


def ring_plan(layer_input, output_grad, expert_ids, route_ints, w_gate, w_up, w_down):
    groups = lax.axis_size("grp")
    members = lax.axis_size("mem")
    tok_rows, model_width = layer_input.shape
    width = w_gate.shape[2]
    span = members * width
    order = ring_order(groups)
    full_steps = (groups - 1) // 2
    has_far = groups % 2 == 0 and groups > 1

    def at_distance(k):
        return [(order[i], order[(i + k) % groups]) for i in range(groups)]

    def shift(array, k):
        return lax.ppermute(array, "grp", at_distance(k))

    def member_shift(array, step):
        return lax.ppermute(array, "mem", [(m, (m + step) % members) for m in range(members)])

    half = tok_rows // 2
    low, high = slice(0, half), slice(half, tok_rows)
    rg, lx = output_grad, layer_input
    rx = {high: layer_input[high], low: layer_input[low]}
    lg = {low: output_grad[low], high: output_grad[high]}
    from_left, from_right = [], []
    for k in range(1, full_steps + 1):
        rg, lx = shift(rg, 1), shift(lx, -1)
        rx = {high: shift(rx[high], 1), low: shift(rx[low], 1)}
        lg = {low: shift(lg[low], -1), high: shift(lg[high], -1)}
        from_left.append((rx, {low: rg[low], high: rg[high]}))
        from_right.append(({low: lx[low], high: lx[high]}, lg, lx))
        from_left[-1] += (rg,)
    far = (shift(lx, -1), shift(rg, 1)) if has_far else None

    quotas = route_ints.astype(jnp.float32)
    route_ratio = quotas / jnp.sum(quotas, axis=1, keepdims=True)
    group_at = jnp.array(
        [[order[(order.index(g) + k) % groups] for k in range(groups)] for g in range(groups)],
        jnp.int32,
    )
    mine = jnp.arange(groups, dtype=jnp.int32)[:, None] == lax.axis_index("grp")
    chip = jnp.sum(jnp.where(mine, group_at, 0), axis=0)
    core = (lax.axis_index("mem") + jnp.arange(members, dtype=jnp.int32)) % members
    expert = chip[:, None] * members + core[None, :]
    chosen = expert_ids[None, None, :, :] == expert[:, :, None, None]
    outgoing = jnp.sum(jnp.where(chosen, route_ratio[None, None], 0.0), axis=3)

    blocks = [outgoing[d] for d in range(groups)]
    for bit in range((groups - 1).bit_length()):
        going = [d for d in range(groups) if d >> bit & 1]
        packed = jnp.concatenate([blocks[d] for d in going], axis=0)
        moved = shift(packed, 1 << bit)
        for i, d in enumerate(going):
            blocks[d] = moved[i * members : (i + 1) * members]

    def ratio_from(distance):
        return blocks[-distance % groups]

    gates, ups, downs = [w_gate[0]], [w_up[0]], [w_down[0]]
    for k in range(1, members):
        gates.append(member_shift(w_gate[0], members - k))
        ups.append(member_shift(w_up[0], members - k))
        downs.append(member_shift(w_down[0], members - k))
    gate_w = jnp.concatenate(gates, axis=1)
    up_w = jnp.concatenate(ups, axis=1)
    down_w = jnp.concatenate(downs, axis=0)
    column = jnp.arange(span, dtype=jnp.int32)[None, :] // width

    def piece(x, og, ratio):
        r = ratio[:, 0:1]
        for m in range(1, members):
            r = jnp.where(column == m, ratio[:, m : m + 1], r)
        gate, up = mm(x, gate_w), mm(x, up_w)
        s = jax.nn.sigmoid(gate)
        act = gate * s
        hidden = (act * up * r).astype(jnp.bfloat16)
        hg = r * mm(og, down_w, NT)
        ug = (hg * act).astype(jnp.bfloat16)
        gg = (hg * up * s * (1.0 + gate * (1.0 - s))).astype(jnp.bfloat16)
        part = mm(gg, gate_w, NT) + mm(ug, up_w, NT)
        return part, gg, ug, hidden

    kept = []

    def step_piece(xs, ogs, ratios, apart=False):
        x, og = jnp.concatenate(xs, axis=0), jnp.concatenate(ogs, axis=0)
        if apart:
            x, og = lax.optimization_barrier((x, og))
        ratio = jnp.concatenate(ratios, axis=1).T
        if kept:
            ratio = lax.optimization_barrier((ratio, kept[-1][2]))[0]
        part, *rest = piece(x, og, ratio)
        kept.append((x, og, *rest))
        return part.astype(jnp.bfloat16)

    parts = {}
    for k in range(1, full_steps):
        lefts, rights = from_left[k - 1], from_right[k - 1]
        xs = [lefts[0][low], lefts[0][high], rights[2]]
        ogs = [lefts[2], rights[1][low], rights[1][high]]
        ratio = [ratio_from(-k), ratio_from(k)]
        if k == 1:
            xs, ogs, ratio = xs + [layer_input], ogs + [output_grad], ratio + [outgoing[0]]
        part = step_piece(xs, ogs, ratio)
        parts[k] = [
            {rows: part[at + rows.start : at + rows.stop] for rows in (low, high)}
            for at in (0, tok_rows)
        ]
        if k == 1:
            own_part = part[2 * tok_rows :]
    if full_steps < 2:
        own_part = step_piece([layer_input], [output_grad], [outgoing[0]])
    if has_far:
        far_part = step_piece([far[0]], [far[1]], [ratio_from(groups // 2)])
    if full_steps:
        k = full_steps
        lefts, rights = from_left[k - 1], from_right[k - 1]
        parts[k] = [{}, {}]
        for one, two in ((high, low), (low, high)):
            ratio = [ratio_from(-k)[:, one], ratio_from(k)[:, two]]
            part = step_piece(
                [lefts[0][one], rights[0][two]], [lefts[1][one], rights[1][two]], ratio, apart=True
            )
            parts[k][0][one], parts[k][1][two] = part[:half], part[half:]

    def join(moved, part):
        return (moved.astype(jnp.float32) + part.astype(jnp.float32)).astype(jnp.bfloat16)

    def send(pair):
        return shift(pair[0], -1), shift(pair[1], 1)

    def parts_at(k, rows):
        return parts[k][0][rows[0]], parts[k][1][rows[1]]

    long_rows, short_rows = (low, high), (high, low)
    long_way = short_way = before = None

    def gated(pair):
        return pair if before is None else lax.optimization_barrier((pair, before))[0]

    if has_far:
        long_way = send((far_part[low], far_part[high]))
    for k in reversed(range(1, full_steps + 1)):
        sums = parts_at(k, short_rows)
        if short_way is not None:
            sums = before = tuple(map(join, short_way, gated(sums)))
        short_way = send(sums)
        sums = parts_at(k, long_rows)
        if long_way is not None:
            sums = before = tuple(map(join, long_way, gated(sums)))
        long_way = send(sums)
    back_low = [long_way and long_way[0], short_way and short_way[1]]
    back_high = [long_way and long_way[1], short_way and short_way[0]]

    def closing(rows, returned):
        total = own_part[rows].astype(jnp.float32)
        for piece_back in returned:
            if piece_back is not None:
                total = total + piece_back.astype(jnp.float32)
        return total.astype(jnp.bfloat16)

    input_grad = jnp.zeros((tok_rows, model_width), jnp.bfloat16)
    input_grad = lax.dynamic_update_slice(input_grad, closing(low, back_low), (0, 0))
    input_grad = lax.dynamic_update_slice(input_grad, closing(high, back_high), (half, 0))

    x_all, og_all, gg_all, ug_all, hidden_all = (
        jnp.concatenate([k[i] for k in kept], axis=0) for i in range(5)
    )

    def member_sum(product, axis):
        both = lax.optimization_barrier(product.astype(jnp.bfloat16))
        blocks = jnp.split(both, members, axis=axis)
        moved = [member_shift(blocks[k], k) for k in range(1, members)]
        total = sum(block.astype(jnp.float32) for block in [blocks[0], *moved])
        return total.astype(jnp.bfloat16)[None]

    gate_p = mm(x_all, gg_all, TN)
    up_p = mm(x_all, ug_all, TN)
    down_p = mm(hidden_all, og_all, TN)
    gate_g = member_sum(gate_p, 1)
    up_g = member_sum(up_p, 1)
    down_g = member_sum(down_p, 0)
    return (input_grad, gate_g, up_g, down_g)


def local(layer_input, output_grad, expert_ids, route_ints, w_gate, w_up, w_down):
    devices = lax.axis_size("grp") * lax.axis_size("mem")
    tok_rows, top_count = expert_ids.shape
    capacity = max(2, 9 * tok_rows * top_count // (8 * devices))
    plan = ring_plan if tok_rows <= 2 * capacity else exchange_plan
    return plan(layer_input, output_grad, expert_ids, route_ints, w_gate, w_up, w_down)


def solution(mesh):
    return jax.shard_map(
        local,
        mesh=mesh,
        in_specs=(
            P(("rep", "grp", "mem"), None),
            P(("rep", "grp", "mem"), None),
            P(("rep", "grp", "mem"), None),
            P(("rep", "grp", "mem"), None),
            P(("grp", "mem"), None, None),
            P(("grp", "mem"), None, None),
            P(("grp", "mem"), None, None),
        ),
        out_specs=(
            P(("rep", "grp", "mem"), None),
            P(("rep", "grp", "mem"), None, None),
            P(("rep", "grp", "mem"), None, None),
            P(("rep", "grp", "mem"), None, None),
        ),
        check_vma=False,
    )
```

```python
import jax
import jax.numpy as jnp
from jax import lax
from jax.sharding import PartitionSpec as P


def exchange_plan(layer_input, output_grad, expert_ids, route_ints, w_gate, w_up, w_down):
    devices = lax.axis_size("grp") * lax.axis_size("mem")
    tok_rows = layer_input.shape[0]
    model_width = layer_input.shape[1]
    top_count = expert_ids.shape[1]
    pair_count = tok_rows * top_count
    capacity = max(2, 9 * tok_rows * top_count // (8 * devices))
    slot_count = devices * capacity
    quotas = route_ints.astype(jnp.float32)
    route_ratio = quotas / jnp.sum(quotas, axis=1, keepdims=True)
    scaled = (route_ratio[:, :, None] * output_grad.astype(jnp.float32)[:, None, :]).astype(
        jnp.bfloat16
    )
    scaled = scaled.reshape(pair_count, model_width)
    flat_ids = expert_ids.reshape(pair_count)
    pair_order = jnp.arange(pair_count, dtype=jnp.int32)
    earlier = (flat_ids[None, :] == flat_ids[:, None]) & (pair_order[None, :] < pair_order[:, None])
    slot_rank = jnp.sum(earlier.astype(jnp.int32), axis=1)
    slot_key = flat_ids * capacity + slot_rank
    slot_match = slot_key[None, :] == jnp.arange(slot_count, dtype=jnp.int32)[:, None]
    filled = jnp.any(slot_match, axis=1)
    source_pair = jnp.sum(jnp.where(slot_match, pair_order[None, :], 0), axis=1)
    send_x = jnp.where(
        filled[:, None], layer_input[source_pair // top_count], jnp.zeros((), jnp.bfloat16)
    )
    send_grad = jnp.where(filled[:, None], scaled[source_pair], jnp.zeros((), jnp.bfloat16))
    recv_x, recv_grad = (
        lax.all_to_all(
            send_x.reshape(devices, capacity, model_width),
            ("grp", "mem"),
            split_axis=0,
            concat_axis=0,
            tiled=True,
        ),
        lax.all_to_all(
            send_grad.reshape(devices, capacity, model_width),
            ("grp", "mem"),
            split_axis=0,
            concat_axis=0,
            tiled=True,
        ),
    )
    rows_x = recv_x.reshape(slot_count, model_width)
    rows_grad = recv_grad.reshape(slot_count, model_width)
    gate_w = w_gate[0]
    up_w = w_up[0]
    down_w = w_down[0]
    gate_pre = jnp.dot(rows_x, gate_w, preferred_element_type=jnp.float32)
    up_pre = jnp.dot(rows_x, up_w, preferred_element_type=jnp.float32)
    sigmoid_gate = jax.nn.sigmoid(gate_pre)
    activity = gate_pre * sigmoid_gate
    hidden = (activity * up_pre).astype(jnp.bfloat16)
    hidden_grad = jnp.dot(rows_grad, down_w.T, preferred_element_type=jnp.float32)
    up_grad = (hidden_grad * activity).astype(jnp.bfloat16)
    gate_grad = (
        hidden_grad * up_pre * sigmoid_gate * (1.0 + gate_pre * (1.0 - sigmoid_gate))
    ).astype(jnp.bfloat16)
    row_grad = (
        jnp.dot(gate_grad, gate_w.T, preferred_element_type=jnp.float32)
        + jnp.dot(up_grad, up_w.T, preferred_element_type=jnp.float32)
    ).astype(jnp.bfloat16)
    returned = lax.all_to_all(
        row_grad.reshape(devices, capacity, model_width),
        ("grp", "mem"),
        split_axis=0,
        concat_axis=0,
        tiled=True,
    )
    down_wgrad = jnp.dot(hidden.T, rows_grad, preferred_element_type=jnp.float32).astype(
        jnp.bfloat16
    )
    gate_wgrad = jnp.dot(rows_x.T, gate_grad, preferred_element_type=jnp.float32).astype(
        jnp.bfloat16
    )
    up_wgrad = jnp.dot(rows_x.T, up_grad, preferred_element_type=jnp.float32).astype(jnp.bfloat16)
    back_rows = returned.reshape(slot_count, model_width)
    pair_rows = back_rows[slot_key].reshape(tok_rows, top_count, model_width)
    input_grad = jnp.sum(pair_rows.astype(jnp.float32), axis=1).astype(jnp.bfloat16)
    return (input_grad, gate_wgrad[None], up_wgrad[None], down_wgrad[None])


TN = (((0,), (0,)), ((), ()))
NT = (((1,), (1,)), ((), ()))


def ring_order(count):
    return list(range(0, count, 2)) + list(reversed(range(1, count, 2)))


def mm(a, b, dims=(((1,), (0,)), ((), ()))):
    return lax.dot_general(a, b, dims, preferred_element_type=jnp.float32)


def ring_plan(layer_input, output_grad, expert_ids, route_ints, w_gate, w_up, w_down):
    groups = lax.axis_size("grp")
    members = lax.axis_size("mem")
    tok_rows, model_width = layer_input.shape
    width = w_gate.shape[2]
    span = members * width
    order = ring_order(groups)
    full_steps = (groups - 1) // 2
    has_far = groups % 2 == 0 and groups > 1

    def at_distance(k):
        return [(order[i], order[(i + k) % groups]) for i in range(groups)]

    def shift(array, k):
        return lax.ppermute(array, "grp", at_distance(k))

    def member_shift(array, step):
        return lax.ppermute(array, "mem", [(m, (m + step) % members) for m in range(members)])

    half = tok_rows // 2
    low, high = slice(0, half), slice(half, tok_rows)
    rg, lx = output_grad, layer_input
    rx = {high: layer_input[high], low: layer_input[low]}
    lg = {low: output_grad[low], high: output_grad[high]}
    from_left, from_right = [], []
    for k in range(1, full_steps + 1):
        rg, lx = shift(rg, 1), shift(lx, -1)
        rx = {high: shift(rx[high], 1), low: shift(rx[low], 1)}
        lg = {low: shift(lg[low], -1), high: shift(lg[high], -1)}
        from_left.append((rx, {low: rg[low], high: rg[high]}))
        from_right.append(({low: lx[low], high: lx[high]}, lg, lx))
        from_left[-1] += (rg,)
    far = (shift(lx, -1), shift(rg, 1)) if has_far else None

    quotas = route_ints.astype(jnp.float32)
    route_ratio = quotas / jnp.sum(quotas, axis=1, keepdims=True)
    group_at = jnp.array(
        [[order[(order.index(g) + k) % groups] for k in range(groups)] for g in range(groups)],
        jnp.int32,
    )
    mine = jnp.arange(groups, dtype=jnp.int32)[:, None] == lax.axis_index("grp")
    chip = jnp.sum(jnp.where(mine, group_at, 0), axis=0)
    core = (lax.axis_index("mem") + jnp.arange(members, dtype=jnp.int32)) % members
    expert = chip[:, None] * members + core[None, :]
    chosen = expert_ids[None, None, :, :] == expert[:, :, None, None]
    outgoing = jnp.sum(jnp.where(chosen, route_ratio[None, None], 0.0), axis=3)

    distances = [d for k in range(1, full_steps + 1) for d in (k, -k)] + [groups // 2] * has_far
    blocks = {d: outgoing[d % groups] for d in distances}
    for bit in range((groups // 2).bit_length()):
        for sign in (1, -1):
            going = [d for d in distances if d * sign > 0 and abs(d) >> bit & 1]
            if not going:
                continue
            packed = jnp.concatenate([blocks[d] for d in going], axis=0)
            moved = shift(packed, sign << bit)
            for i, d in enumerate(going):
                blocks[d] = moved[i * members : (i + 1) * members]

    def ratio_from(distance):
        return blocks[-distance]

    gates, ups, downs = [w_gate[0]], [w_up[0]], [w_down[0]]
    for k in range(1, members):
        gates.append(member_shift(w_gate[0], members - k))
        ups.append(member_shift(w_up[0], members - k))
        downs.append(member_shift(w_down[0], members - k))
    gate_w = jnp.concatenate(gates, axis=1)
    up_w = jnp.concatenate(ups, axis=1)
    down_w = jnp.concatenate(downs, axis=0)
    column = jnp.arange(span, dtype=jnp.int32)[None, :] // width

    def piece(x, og, ratio):
        r = ratio[:, 0:1]
        for m in range(1, members):
            r = jnp.where(column == m, ratio[:, m : m + 1], r)
        gate, up = mm(x, gate_w), mm(x, up_w)
        s = jax.nn.sigmoid(gate)
        act = gate * s
        hidden = (act * up * r).astype(jnp.bfloat16)
        hg = r * mm(og, down_w, NT)
        ug = (hg * act).astype(jnp.bfloat16)
        gg = (hg * up * s * (1.0 + gate * (1.0 - s))).astype(jnp.bfloat16)
        part = mm(gg, gate_w, NT) + mm(ug, up_w, NT)
        return part, gg, ug, hidden

    kept = []

    def step_piece(xs, ogs, ratios, apart=False):
        x, og = jnp.concatenate(xs, axis=0), jnp.concatenate(ogs, axis=0)
        if apart:
            x, og = lax.optimization_barrier((x, og))
        ratio = jnp.concatenate(ratios, axis=1).T
        if kept:
            ratio = lax.optimization_barrier((ratio, kept[-1][2]))[0]
        part, *rest = piece(x, og, ratio)
        kept.append((x, og, *rest))
        return part.astype(jnp.bfloat16)

    parts = {}
    for k in range(1, full_steps):
        lefts, rights = from_left[k - 1], from_right[k - 1]
        xs = [lefts[0][low], lefts[0][high], rights[2]]
        ogs = [lefts[2], rights[1][low], rights[1][high]]
        ratio = [ratio_from(-k), ratio_from(k)]
        if k == 1:
            xs, ogs, ratio = xs + [layer_input], ogs + [output_grad], ratio + [outgoing[0]]
        part = step_piece(xs, ogs, ratio)
        parts[k] = [
            {rows: part[at + rows.start : at + rows.stop] for rows in (low, high)}
            for at in (0, tok_rows)
        ]
        if k == 1:
            own_part = part[2 * tok_rows :]
    if full_steps < 2:
        own_part = step_piece([layer_input], [output_grad], [outgoing[0]])

    def far_piece():
        return step_piece([far[0]], [far[1]], [blocks[groups // 2]]) if has_far else None

    if full_steps:
        k = full_steps
        lefts, rights = from_left[k - 1], from_right[k - 1]
        parts[k] = [{}, {}]
        for name, one, two in (("a", high, low), ("b", low, high)):
            if name == "b":
                far_part = far_piece()
            ratio = [ratio_from(-k)[:, one], ratio_from(k)[:, two]]
            part = step_piece(
                [lefts[0][one], rights[0][two]], [lefts[1][one], rights[1][two]], ratio, apart=True
            )
            parts[k][0][one], parts[k][1][two] = part[:half], part[half:]
    else:
        far_part = far_piece()

    def join(moved, part):
        return (moved.astype(jnp.float32) + part.astype(jnp.float32)).astype(jnp.bfloat16)

    def send(pair):
        return shift(pair[0], -1), shift(pair[1], 1)

    def parts_at(k, rows):
        return parts[k][0][rows[0]], parts[k][1][rows[1]]

    long_rows, short_rows = (low, high), (high, low)
    long_way = short_way = before = None

    def gated(pair):
        return pair if before is None else lax.optimization_barrier((pair, before))[0]

    if has_far:
        long_way = send((far_part[low], far_part[high]))
    for k in reversed(range(1, full_steps + 1)):
        sums = parts_at(k, short_rows)
        if short_way is not None:
            sums = before = tuple(map(join, short_way, gated(sums)))
        short_way = send(sums)
        sums = parts_at(k, long_rows)
        if long_way is not None:
            sums = before = tuple(map(join, long_way, gated(sums)))
        long_way = send(sums)
    back_low = [long_way and long_way[0], short_way and short_way[1]]
    back_high = [long_way and long_way[1], short_way and short_way[0]]

    def closing(rows, returned):
        total = own_part[rows].astype(jnp.float32)
        for piece_back in returned:
            if piece_back is not None:
                total = total + piece_back.astype(jnp.float32)
        return total.astype(jnp.bfloat16)

    input_grad = jnp.zeros((tok_rows, model_width), jnp.bfloat16)
    input_grad = lax.dynamic_update_slice(input_grad, closing(low, back_low), (0, 0))
    input_grad = lax.dynamic_update_slice(input_grad, closing(high, back_high), (half, 0))

    x_all, og_all, gg_all, ug_all, hidden_all = (
        jnp.concatenate([k[i] for k in kept], axis=0) for i in range(5)
    )

    def member_sum(product, axis):
        both = lax.optimization_barrier(product.astype(jnp.bfloat16))
        blocks = jnp.split(both, members, axis=axis)
        moved = [member_shift(blocks[k], k) for k in range(1, members)]
        total = sum(block.astype(jnp.float32) for block in [blocks[0], *moved])
        return total.astype(jnp.bfloat16)[None]

    gate_p = mm(x_all, gg_all, TN)
    up_p = mm(x_all, ug_all, TN)
    down_p = mm(hidden_all, og_all, TN)
    gate_g = member_sum(gate_p, 1)
    up_g = member_sum(up_p, 1)
    down_g = member_sum(down_p, 0)
    return (input_grad, gate_g, up_g, down_g)


def local(layer_input, output_grad, expert_ids, route_ints, w_gate, w_up, w_down):
    devices = lax.axis_size("grp") * lax.axis_size("mem")
    tok_rows, top_count = expert_ids.shape
    capacity = max(2, 9 * tok_rows * top_count // (8 * devices))
    plan = ring_plan if tok_rows <= 2 * capacity else exchange_plan
    return plan(layer_input, output_grad, expert_ids, route_ints, w_gate, w_up, w_down)


def solution(mesh):
    return jax.shard_map(
        local,
        mesh=mesh,
        in_specs=(
            P(("rep", "grp", "mem"), None),
            P(("rep", "grp", "mem"), None),
            P(("rep", "grp", "mem"), None),
            P(("rep", "grp", "mem"), None),
            P(("grp", "mem"), None, None),
            P(("grp", "mem"), None, None),
            P(("grp", "mem"), None, None),
        ),
        out_specs=(
            P(("rep", "grp", "mem"), None),
            P(("rep", "grp", "mem"), None, None),
            P(("rep", "grp", "mem"), None, None),
            P(("rep", "grp", "mem"), None, None),
        ),
        check_vma=False,
    )
```

```python
import jax
import jax.numpy as jnp
from jax import lax
from jax.sharding import PartitionSpec as P


def exchange_plan(layer_input, output_grad, expert_ids, route_ints, w_gate, w_up, w_down):
    devices = lax.axis_size("grp") * lax.axis_size("mem")
    tok_rows = layer_input.shape[0]
    model_width = layer_input.shape[1]
    top_count = expert_ids.shape[1]
    pair_count = tok_rows * top_count
    capacity = max(2, 9 * tok_rows * top_count // (8 * devices))
    slot_count = devices * capacity
    quotas = route_ints.astype(jnp.float32)
    route_ratio = quotas / jnp.sum(quotas, axis=1, keepdims=True)
    scaled = (route_ratio[:, :, None] * output_grad.astype(jnp.float32)[:, None, :]).astype(
        jnp.bfloat16
    )
    scaled = scaled.reshape(pair_count, model_width)
    flat_ids = expert_ids.reshape(pair_count)
    pair_order = jnp.arange(pair_count, dtype=jnp.int32)
    earlier = (flat_ids[None, :] == flat_ids[:, None]) & (pair_order[None, :] < pair_order[:, None])
    slot_rank = jnp.sum(earlier.astype(jnp.int32), axis=1)
    slot_key = flat_ids * capacity + slot_rank
    slot_match = slot_key[None, :] == jnp.arange(slot_count, dtype=jnp.int32)[:, None]
    filled = jnp.any(slot_match, axis=1)
    source_pair = jnp.sum(jnp.where(slot_match, pair_order[None, :], 0), axis=1)
    send_x = jnp.where(
        filled[:, None], layer_input[source_pair // top_count], jnp.zeros((), jnp.bfloat16)
    )
    send_grad = jnp.where(filled[:, None], scaled[source_pair], jnp.zeros((), jnp.bfloat16))
    recv_x, recv_grad = (
        lax.all_to_all(
            send_x.reshape(devices, capacity, model_width),
            ("grp", "mem"),
            split_axis=0,
            concat_axis=0,
            tiled=True,
        ),
        lax.all_to_all(
            send_grad.reshape(devices, capacity, model_width),
            ("grp", "mem"),
            split_axis=0,
            concat_axis=0,
            tiled=True,
        ),
    )
    rows_x = recv_x.reshape(slot_count, model_width)
    rows_grad = recv_grad.reshape(slot_count, model_width)
    gate_w = w_gate[0]
    up_w = w_up[0]
    down_w = w_down[0]
    gate_pre = jnp.dot(rows_x, gate_w, preferred_element_type=jnp.float32)
    up_pre = jnp.dot(rows_x, up_w, preferred_element_type=jnp.float32)
    sigmoid_gate = jax.nn.sigmoid(gate_pre)
    activity = gate_pre * sigmoid_gate
    hidden = (activity * up_pre).astype(jnp.bfloat16)
    hidden_grad = jnp.dot(rows_grad, down_w.T, preferred_element_type=jnp.float32)
    up_grad = (hidden_grad * activity).astype(jnp.bfloat16)
    gate_grad = (
        hidden_grad * up_pre * sigmoid_gate * (1.0 + gate_pre * (1.0 - sigmoid_gate))
    ).astype(jnp.bfloat16)
    row_grad = (
        jnp.dot(gate_grad, gate_w.T, preferred_element_type=jnp.float32)
        + jnp.dot(up_grad, up_w.T, preferred_element_type=jnp.float32)
    ).astype(jnp.bfloat16)
    returned = lax.all_to_all(
        row_grad.reshape(devices, capacity, model_width),
        ("grp", "mem"),
        split_axis=0,
        concat_axis=0,
        tiled=True,
    )
    down_wgrad = jnp.dot(hidden.T, rows_grad, preferred_element_type=jnp.float32).astype(
        jnp.bfloat16
    )
    gate_wgrad = jnp.dot(rows_x.T, gate_grad, preferred_element_type=jnp.float32).astype(
        jnp.bfloat16
    )
    up_wgrad = jnp.dot(rows_x.T, up_grad, preferred_element_type=jnp.float32).astype(jnp.bfloat16)
    back_rows = returned.reshape(slot_count, model_width)
    pair_rows = back_rows[slot_key].reshape(tok_rows, top_count, model_width)
    input_grad = jnp.sum(pair_rows.astype(jnp.float32), axis=1).astype(jnp.bfloat16)
    return (input_grad, gate_wgrad[None], up_wgrad[None], down_wgrad[None])


TN = (((0,), (0,)), ((), ()))
NT = (((1,), (1,)), ((), ()))


def ring_order(count):
    return list(range(0, count, 2)) + list(reversed(range(1, count, 2)))


def mm(a, b, dims=(((1,), (0,)), ((), ()))):
    return lax.dot_general(a, b, dims, preferred_element_type=jnp.float32)


def ring_plan(layer_input, output_grad, expert_ids, route_ints, w_gate, w_up, w_down):
    groups = lax.axis_size("grp")
    members = lax.axis_size("mem")
    tok_rows, model_width = layer_input.shape
    width = w_gate.shape[2]
    span = members * width
    order = ring_order(groups)
    full_steps = (groups - 1) // 2
    has_far = groups % 2 == 0 and groups > 1

    def at_distance(k):
        return [(order[i], order[(i + k) % groups]) for i in range(groups)]

    def shift(array, k):
        return lax.ppermute(array, "grp", at_distance(k))

    def member_shift(array, step):
        return lax.ppermute(array, "mem", [(m, (m + step) % members) for m in range(members)])

    half = tok_rows // 2
    low, high = slice(0, half), slice(half, tok_rows)
    rg, lx = output_grad, layer_input
    rx = {high: layer_input[high], low: layer_input[low]}
    lg = {low: output_grad[low], high: output_grad[high]}
    from_left, from_right = [], []
    for k in range(1, full_steps + 1):
        rg, lx = shift(rg, 1), shift(lx, -1)
        rx = {high: shift(rx[high], 1), low: shift(rx[low], 1)}
        lg = {low: shift(lg[low], -1), high: shift(lg[high], -1)}
        from_left.append((rx, {low: rg[low], high: rg[high]}))
        from_right.append(({low: lx[low], high: lx[high]}, lg, lx))
        from_left[-1] += (rg,)
    far = (shift(lx, -1), shift(rg, 1)) if has_far else None

    quotas = route_ints.astype(jnp.float32)
    route_ratio = quotas / jnp.sum(quotas, axis=1, keepdims=True)
    group_at = jnp.array(
        [[order[(order.index(g) + k) % groups] for k in range(groups)] for g in range(groups)],
        jnp.int32,
    )
    mine = jnp.arange(groups, dtype=jnp.int32)[:, None] == lax.axis_index("grp")
    chip = jnp.sum(jnp.where(mine, group_at, 0), axis=0)
    core = (lax.axis_index("mem") + jnp.arange(members, dtype=jnp.int32)) % members
    expert = chip[:, None] * members + core[None, :]
    chosen = expert_ids[None, None, :, :] == expert[:, :, None, None]
    outgoing = jnp.sum(jnp.where(chosen, route_ratio[None, None], 0.0), axis=3)

    distances = [d for k in range(1, full_steps + 1) for d in (k, -k)] + [groups // 2] * has_far
    blocks = {d: outgoing[d % groups] for d in distances}
    for bit in range((groups // 2).bit_length()):
        for sign in (1, -1):
            going = [d for d in distances if d * sign > 0 and abs(d) >> bit & 1]
            if not going:
                continue
            packed = jnp.concatenate([blocks[d] for d in going], axis=0)
            moved = shift(packed, sign << bit)
            for i, d in enumerate(going):
                blocks[d] = moved[i * members : (i + 1) * members]

    def ratio_from(distance):
        return blocks[-distance]

    gates, ups, downs = [w_gate[0]], [w_up[0]], [w_down[0]]
    for k in range(1, members):
        gates.append(member_shift(w_gate[0], members - k))
        ups.append(member_shift(w_up[0], members - k))
        downs.append(member_shift(w_down[0], members - k))
    gate_w = jnp.concatenate(gates, axis=1)
    up_w = jnp.concatenate(ups, axis=1)
    down_w = jnp.concatenate(downs, axis=0)
    column = jnp.arange(span, dtype=jnp.int32)[None, :] // width

    def piece(x, og, ratio):
        r = ratio[:, 0:1]
        for m in range(1, members):
            r = jnp.where(column == m, ratio[:, m : m + 1], r)
        gate, up = mm(x, gate_w), mm(x, up_w)
        s = jax.nn.sigmoid(gate)
        act = gate * s
        hidden = (act * up * r).astype(jnp.bfloat16)
        hg = r * mm(og, down_w, NT)
        ug = (hg * act).astype(jnp.bfloat16)
        gg = (hg * up * s * (1.0 + gate * (1.0 - s))).astype(jnp.bfloat16)
        part = mm(gg, gate_w, NT) + mm(ug, up_w, NT)
        return part, gg, ug, hidden

    kept = []

    def step_piece(xs, ogs, ratios, apart=False):
        x, og = jnp.concatenate(xs, axis=0), jnp.concatenate(ogs, axis=0)
        if apart:
            x, og = lax.optimization_barrier((x, og))
        ratio = jnp.concatenate(ratios, axis=1).T
        if kept:
            ratio = lax.optimization_barrier((ratio, kept[-1][2]))[0]
        part, *rest = piece(x, og, ratio)
        kept.append((x, og, *rest))
        return part.astype(jnp.bfloat16)

    parts = {}
    for k in range(1, full_steps):
        lefts, rights = from_left[k - 1], from_right[k - 1]
        xs = [lefts[0][low], lefts[0][high], rights[2]]
        ogs = [lefts[2], rights[1][low], rights[1][high]]
        ratio = [ratio_from(-k), ratio_from(k)]
        if k == 1:
            xs, ogs, ratio = xs + [layer_input], ogs + [output_grad], ratio + [outgoing[0]]
        part = step_piece(xs, ogs, ratio)
        parts[k] = [
            {rows: part[at + rows.start : at + rows.stop] for rows in (low, high)}
            for at in (0, tok_rows)
        ]
        if k == 1:
            own_part = part[2 * tok_rows :]
    if full_steps < 2:
        own_part = step_piece([layer_input], [output_grad], [outgoing[0]])

    def far_piece():
        return step_piece([far[0]], [far[1]], [blocks[groups // 2]]) if has_far else None

    far_part = far_piece()
    if full_steps:
        k = full_steps
        lefts, rights = from_left[k - 1], from_right[k - 1]
        parts[k] = [{}, {}]
        for one, two in ((high, low), (low, high)):
            ratio = [ratio_from(-k)[:, one], ratio_from(k)[:, two]]
            part = step_piece(
                [lefts[0][one], rights[0][two]], [lefts[1][one], rights[1][two]], ratio, apart=True
            )
            parts[k][0][one], parts[k][1][two] = part[:half], part[half:]

    def join(moved, part):
        return (moved.astype(jnp.float32) + part.astype(jnp.float32)).astype(jnp.bfloat16)

    def send(pair):
        return shift(pair[0], -1), shift(pair[1], 1)

    def parts_at(k, rows):
        return parts[k][0][rows[0]], parts[k][1][rows[1]]

    long_rows, short_rows = (low, high), (high, low)
    long_way = short_way = before = None

    def gated(pair):
        return pair if before is None else lax.optimization_barrier((pair, before))[0]

    if has_far:
        long_way = send((far_part[low], far_part[high]))
    for k in reversed(range(1, full_steps + 1)):
        sums = parts_at(k, short_rows)
        if short_way is not None:
            sums = before = tuple(map(join, short_way, gated(sums)))
        short_way = send(sums)
        sums = parts_at(k, long_rows)
        if long_way is not None:
            sums = before = tuple(map(join, long_way, gated(sums)))
        long_way = send(sums)
    back_low = [long_way and long_way[0], short_way and short_way[1]]
    back_high = [long_way and long_way[1], short_way and short_way[0]]

    def closing(rows, returned):
        total = own_part[rows].astype(jnp.float32)
        for piece_back in returned:
            if piece_back is not None:
                total = total + piece_back.astype(jnp.float32)
        return total.astype(jnp.bfloat16)

    input_grad = jnp.zeros((tok_rows, model_width), jnp.bfloat16)
    input_grad = lax.dynamic_update_slice(input_grad, closing(low, back_low), (0, 0))
    input_grad = lax.dynamic_update_slice(input_grad, closing(high, back_high), (half, 0))

    x_all, og_all, gg_all, ug_all, hidden_all = (
        jnp.concatenate([k[i] for k in kept], axis=0) for i in range(5)
    )

    def member_sum(product, axis):
        both = lax.optimization_barrier(product.astype(jnp.bfloat16))
        blocks = jnp.split(both, members, axis=axis)
        moved = [member_shift(blocks[k], k) for k in range(1, members)]
        total = sum(block.astype(jnp.float32) for block in [blocks[0], *moved])
        return total.astype(jnp.bfloat16)[None]

    gate_p = mm(x_all, gg_all, TN)
    up_p = mm(x_all, ug_all, TN)
    down_p = mm(hidden_all, og_all, TN)
    gate_g = member_sum(gate_p, 1)
    up_g = member_sum(up_p, 1)
    down_g = member_sum(down_p, 0)
    return (input_grad, gate_g, up_g, down_g)


def local(layer_input, output_grad, expert_ids, route_ints, w_gate, w_up, w_down):
    devices = lax.axis_size("grp") * lax.axis_size("mem")
    tok_rows, top_count = expert_ids.shape
    capacity = max(2, 9 * tok_rows * top_count // (8 * devices))
    plan = ring_plan if tok_rows <= 2 * capacity else exchange_plan
    return plan(layer_input, output_grad, expert_ids, route_ints, w_gate, w_up, w_down)


def solution(mesh):
    return jax.shard_map(
        local,
        mesh=mesh,
        in_specs=(
            P(("rep", "grp", "mem"), None),
            P(("rep", "grp", "mem"), None),
            P(("rep", "grp", "mem"), None),
            P(("rep", "grp", "mem"), None),
            P(("grp", "mem"), None, None),
            P(("grp", "mem"), None, None),
            P(("grp", "mem"), None, None),
        ),
        out_specs=(
            P(("rep", "grp", "mem"), None),
            P(("rep", "grp", "mem"), None, None),
            P(("rep", "grp", "mem"), None, None),
            P(("rep", "grp", "mem"), None, None),
        ),
        check_vma=False,
    )
```

```python
import jax
import jax.numpy as jnp
from jax import lax
from jax.sharding import PartitionSpec as P


def exchange_plan(layer_input, output_grad, expert_ids, route_ints, w_gate, w_up, w_down):
    devices = lax.axis_size("grp") * lax.axis_size("mem")
    tok_rows = layer_input.shape[0]
    model_width = layer_input.shape[1]
    top_count = expert_ids.shape[1]
    pair_count = tok_rows * top_count
    capacity = max(2, 9 * tok_rows * top_count // (8 * devices))
    slot_count = devices * capacity
    quotas = route_ints.astype(jnp.float32)
    route_ratio = quotas / jnp.sum(quotas, axis=1, keepdims=True)
    scaled = (route_ratio[:, :, None] * output_grad.astype(jnp.float32)[:, None, :]).astype(
        jnp.bfloat16
    )
    scaled = scaled.reshape(pair_count, model_width)
    flat_ids = expert_ids.reshape(pair_count)
    pair_order = jnp.arange(pair_count, dtype=jnp.int32)
    earlier = (flat_ids[None, :] == flat_ids[:, None]) & (pair_order[None, :] < pair_order[:, None])
    slot_rank = jnp.sum(earlier.astype(jnp.int32), axis=1)
    slot_key = flat_ids * capacity + slot_rank
    slot_match = slot_key[None, :] == jnp.arange(slot_count, dtype=jnp.int32)[:, None]
    filled = jnp.any(slot_match, axis=1)
    source_pair = jnp.sum(jnp.where(slot_match, pair_order[None, :], 0), axis=1)
    send_x = jnp.where(
        filled[:, None], layer_input[source_pair // top_count], jnp.zeros((), jnp.bfloat16)
    )
    send_grad = jnp.where(filled[:, None], scaled[source_pair], jnp.zeros((), jnp.bfloat16))
    recv_x, recv_grad = (
        lax.all_to_all(
            send_x.reshape(devices, capacity, model_width),
            ("grp", "mem"),
            split_axis=0,
            concat_axis=0,
            tiled=True,
        ),
        lax.all_to_all(
            send_grad.reshape(devices, capacity, model_width),
            ("grp", "mem"),
            split_axis=0,
            concat_axis=0,
            tiled=True,
        ),
    )
    rows_x = recv_x.reshape(slot_count, model_width)
    rows_grad = recv_grad.reshape(slot_count, model_width)
    gate_w = w_gate[0]
    up_w = w_up[0]
    down_w = w_down[0]
    gate_pre = jnp.dot(rows_x, gate_w, preferred_element_type=jnp.float32)
    up_pre = jnp.dot(rows_x, up_w, preferred_element_type=jnp.float32)
    sigmoid_gate = jax.nn.sigmoid(gate_pre)
    activity = gate_pre * sigmoid_gate
    hidden = (activity * up_pre).astype(jnp.bfloat16)
    hidden_grad = jnp.dot(rows_grad, down_w.T, preferred_element_type=jnp.float32)
    up_grad = (hidden_grad * activity).astype(jnp.bfloat16)
    gate_grad = (
        hidden_grad * up_pre * sigmoid_gate * (1.0 + gate_pre * (1.0 - sigmoid_gate))
    ).astype(jnp.bfloat16)
    row_grad = (
        jnp.dot(gate_grad, gate_w.T, preferred_element_type=jnp.float32)
        + jnp.dot(up_grad, up_w.T, preferred_element_type=jnp.float32)
    ).astype(jnp.bfloat16)
    returned = lax.all_to_all(
        row_grad.reshape(devices, capacity, model_width),
        ("grp", "mem"),
        split_axis=0,
        concat_axis=0,
        tiled=True,
    )
    down_wgrad = jnp.dot(hidden.T, rows_grad, preferred_element_type=jnp.float32).astype(
        jnp.bfloat16
    )
    gate_wgrad = jnp.dot(rows_x.T, gate_grad, preferred_element_type=jnp.float32).astype(
        jnp.bfloat16
    )
    up_wgrad = jnp.dot(rows_x.T, up_grad, preferred_element_type=jnp.float32).astype(jnp.bfloat16)
    back_rows = returned.reshape(slot_count, model_width)
    pair_rows = back_rows[slot_key].reshape(tok_rows, top_count, model_width)
    input_grad = jnp.sum(pair_rows.astype(jnp.float32), axis=1).astype(jnp.bfloat16)
    return (input_grad, gate_wgrad[None], up_wgrad[None], down_wgrad[None])


TN = (((0,), (0,)), ((), ()))
NT = (((1,), (1,)), ((), ()))


def ring_order(count):
    return list(range(0, count, 2)) + list(reversed(range(1, count, 2)))


def mm(a, b, dims=(((1,), (0,)), ((), ()))):
    return lax.dot_general(a, b, dims, preferred_element_type=jnp.float32)


def ring_plan(layer_input, output_grad, expert_ids, route_ints, w_gate, w_up, w_down):
    groups = lax.axis_size("grp")
    members = lax.axis_size("mem")
    tok_rows, model_width = layer_input.shape
    width = w_gate.shape[2]
    span = members * width
    order = ring_order(groups)
    full_steps = (groups - 1) // 2
    has_far = groups % 2 == 0 and groups > 1

    def at_distance(k):
        return [(order[i], order[(i + k) % groups]) for i in range(groups)]

    def shift(array, k):
        return lax.ppermute(array, "grp", at_distance(k))

    def member_shift(array, step):
        return lax.ppermute(array, "mem", [(m, (m + step) % members) for m in range(members)])

    half = tok_rows // 2
    low, high = slice(0, half), slice(half, tok_rows)
    rg, lx = output_grad, layer_input
    rx = {high: layer_input[high], low: layer_input[low]}
    lg = {low: output_grad[low], high: output_grad[high]}
    from_left, from_right = [], []
    for k in range(1, full_steps + 1):
        rg, lx = shift(rg, 1), shift(lx, -1)
        rx = {high: shift(rx[high], 1), low: shift(rx[low], 1)}
        lg = {low: shift(lg[low], -1), high: shift(lg[high], -1)}
        from_left.append((rx, {low: rg[low], high: rg[high]}))
        from_right.append(({low: lx[low], high: lx[high]}, lg, lx))
        from_left[-1] += (rg,)
    far = (shift(lx, -1), shift(rg, 1)) if has_far else None

    quotas = route_ints.astype(jnp.float32)
    route_ratio = quotas / jnp.sum(quotas, axis=1, keepdims=True)
    group_at = jnp.array(
        [[order[(order.index(g) + k) % groups] for k in range(groups)] for g in range(groups)],
        jnp.int32,
    )
    mine = jnp.arange(groups, dtype=jnp.int32)[:, None] == lax.axis_index("grp")
    chip = jnp.sum(jnp.where(mine, group_at, 0), axis=0)
    core = (lax.axis_index("mem") + jnp.arange(members, dtype=jnp.int32)) % members
    expert = chip[:, None] * members + core[None, :]
    chosen = expert_ids[None, None, :, :] == expert[:, :, None, None]
    outgoing = jnp.sum(jnp.where(chosen, route_ratio[None, None], 0.0), axis=3)

    distances = [d for k in range(1, full_steps + 1) for d in (k, -k)] + [groups // 2] * has_far
    blocks = {d: outgoing[d % groups] for d in distances}
    for bit in range((groups // 2).bit_length()):
        for sign in (1, -1):
            going = [d for d in distances if d * sign > 0 and abs(d) >> bit & 1]
            if not going:
                continue
            packed = jnp.concatenate([blocks[d] for d in going], axis=0)
            moved = shift(packed, sign << bit)
            for i, d in enumerate(going):
                blocks[d] = moved[i * members : (i + 1) * members]

    def ratio_from(distance):
        return blocks[-distance]

    gates, ups, downs = [w_gate[0]], [w_up[0]], [w_down[0]]
    for k in range(1, members):
        gates.append(member_shift(w_gate[0], members - k))
        ups.append(member_shift(w_up[0], members - k))
        downs.append(member_shift(w_down[0], members - k))
    gate_w = jnp.concatenate(gates, axis=1)
    up_w = jnp.concatenate(ups, axis=1)
    down_w = jnp.concatenate(downs, axis=0)
    column = jnp.arange(span, dtype=jnp.int32)[None, :] // width

    def piece(x, og, ratio):
        r = ratio[:, 0:1]
        for m in range(1, members):
            r = jnp.where(column == m, ratio[:, m : m + 1], r)
        gate, up = mm(x, gate_w), mm(x, up_w)
        s = jax.nn.sigmoid(gate)
        act = gate * s
        hidden = (act * up * r).astype(jnp.bfloat16)
        hg = r * mm(og, down_w, NT)
        ug = (hg * act).astype(jnp.bfloat16)
        gg = (hg * up * s * (1.0 + gate * (1.0 - s))).astype(jnp.bfloat16)
        part = mm(gg, gate_w, NT) + mm(ug, up_w, NT)
        return part, gg, ug, hidden

    kept = []

    def step_piece(xs, ogs, ratios, apart=False):
        x, og = jnp.concatenate(xs, axis=0), jnp.concatenate(ogs, axis=0)
        if apart:
            x, og = lax.optimization_barrier((x, og))
        ratio = jnp.concatenate(ratios, axis=1).T
        if kept:
            ratio = lax.optimization_barrier((ratio, kept[-1][2]))[0]
        part, *rest = piece(x, og, ratio)
        kept.append((x, og, *rest))
        return part.astype(jnp.bfloat16)

    parts = {}

    def whole_step(k):
        lefts, rights = from_left[k - 1], from_right[k - 1]
        xs = [lefts[0][low], lefts[0][high], rights[2]]
        ogs = [lefts[2], rights[1][low], rights[1][high]]
        ratio = [ratio_from(-k), ratio_from(k)]
        if k == 1:
            xs, ogs, ratio = xs + [layer_input], ogs + [output_grad], ratio + [outgoing[0]]
        part = step_piece(xs, ogs, ratio)
        parts[k] = [
            {rows: part[at + rows.start : at + rows.stop] for rows in (low, high)}
            for at in (0, tok_rows)
        ]
        return part[2 * tok_rows :]

    own_part = None
    for k in range(1, full_steps - 1):
        own_part = whole_step(k) if k == 1 else (whole_step(k), own_part)[1]
    if full_steps < 2:
        own_part = step_piece([layer_input], [output_grad], [outgoing[0]])

    def far_piece():
        return step_piece([far[0]], [far[1]], [blocks[groups // 2]]) if has_far else None

    far_part = far_piece()
    if full_steps > 1:
        rest = whole_step(full_steps - 1)
        own_part = rest if own_part is None else own_part
    if full_steps:
        k = full_steps
        lefts, rights = from_left[k - 1], from_right[k - 1]
        parts[k] = [{}, {}]
        for one, two in ((high, low), (low, high)):
            ratio = [ratio_from(-k)[:, one], ratio_from(k)[:, two]]
            part = step_piece(
                [lefts[0][one], rights[0][two]], [lefts[1][one], rights[1][two]], ratio, apart=True
            )
            parts[k][0][one], parts[k][1][two] = part[:half], part[half:]

    def join(moved, part):
        return (moved.astype(jnp.float32) + part.astype(jnp.float32)).astype(jnp.bfloat16)

    def send(pair):
        return shift(pair[0], -1), shift(pair[1], 1)

    def parts_at(k, rows):
        return parts[k][0][rows[0]], parts[k][1][rows[1]]

    long_rows, short_rows = (low, high), (high, low)
    long_way = short_way = before = None

    def gated(pair):
        return pair if before is None else lax.optimization_barrier((pair, before))[0]

    if has_far:
        long_way = send((far_part[low], far_part[high]))
    for k in reversed(range(1, full_steps + 1)):
        sums = parts_at(k, short_rows)
        if short_way is not None:
            sums = before = tuple(map(join, short_way, gated(sums)))
        short_way = send(sums)
        sums = parts_at(k, long_rows)
        if long_way is not None:
            sums = before = tuple(map(join, long_way, gated(sums)))
        long_way = send(sums)
    back_low = [long_way and long_way[0], short_way and short_way[1]]
    back_high = [long_way and long_way[1], short_way and short_way[0]]

    def closing(rows, returned):
        total = own_part[rows].astype(jnp.float32)
        for piece_back in returned:
            if piece_back is not None:
                total = total + piece_back.astype(jnp.float32)
        return total.astype(jnp.bfloat16)

    input_grad = jnp.zeros((tok_rows, model_width), jnp.bfloat16)
    input_grad = lax.dynamic_update_slice(input_grad, closing(low, back_low), (0, 0))
    input_grad = lax.dynamic_update_slice(input_grad, closing(high, back_high), (half, 0))

    x_all, og_all, gg_all, ug_all, hidden_all = (
        jnp.concatenate([k[i] for k in kept], axis=0) for i in range(5)
    )

    def member_sum(product, axis):
        both = lax.optimization_barrier(product.astype(jnp.bfloat16))
        blocks = jnp.split(both, members, axis=axis)
        moved = [member_shift(blocks[k], k) for k in range(1, members)]
        total = sum(block.astype(jnp.float32) for block in [blocks[0], *moved])
        return total.astype(jnp.bfloat16)[None]

    gate_p = mm(x_all, gg_all, TN)
    up_p = mm(x_all, ug_all, TN)
    down_p = mm(hidden_all, og_all, TN)
    gate_g = member_sum(gate_p, 1)
    up_g = member_sum(up_p, 1)
    down_g = member_sum(down_p, 0)
    return (input_grad, gate_g, up_g, down_g)


def local(layer_input, output_grad, expert_ids, route_ints, w_gate, w_up, w_down):
    devices = lax.axis_size("grp") * lax.axis_size("mem")
    tok_rows, top_count = expert_ids.shape
    capacity = max(2, 9 * tok_rows * top_count // (8 * devices))
    plan = ring_plan if tok_rows <= 2 * capacity else exchange_plan
    return plan(layer_input, output_grad, expert_ids, route_ints, w_gate, w_up, w_down)


def solution(mesh):
    return jax.shard_map(
        local,
        mesh=mesh,
        in_specs=(
            P(("rep", "grp", "mem"), None),
            P(("rep", "grp", "mem"), None),
            P(("rep", "grp", "mem"), None),
            P(("rep", "grp", "mem"), None),
            P(("grp", "mem"), None, None),
            P(("grp", "mem"), None, None),
            P(("grp", "mem"), None, None),
        ),
        out_specs=(
            P(("rep", "grp", "mem"), None),
            P(("rep", "grp", "mem"), None, None),
            P(("rep", "grp", "mem"), None, None),
            P(("rep", "grp", "mem"), None, None),
        ),
        check_vma=False,
    )
```

```python
import jax
import jax.numpy as jnp
from jax import lax
from jax.experimental.layout import Layout, with_layout_constraint
from jax.sharding import PartitionSpec as P


def exchange_plan(layer_input, output_grad, expert_ids, route_ints, w_gate, w_up, w_down):
    devices = lax.axis_size("grp") * lax.axis_size("mem")
    tok_rows = layer_input.shape[0]
    model_width = layer_input.shape[1]
    top_count = expert_ids.shape[1]
    pair_count = tok_rows * top_count
    capacity = max(2, 9 * tok_rows * top_count // (8 * devices))
    slot_count = devices * capacity
    quotas = route_ints.astype(jnp.float32)
    route_ratio = quotas / jnp.sum(quotas, axis=1, keepdims=True)
    scaled = (route_ratio[:, :, None] * output_grad.astype(jnp.float32)[:, None, :]).astype(
        jnp.bfloat16
    )
    scaled = scaled.reshape(pair_count, model_width)
    flat_ids = expert_ids.reshape(pair_count)
    pair_order = jnp.arange(pair_count, dtype=jnp.int32)
    earlier = (flat_ids[None, :] == flat_ids[:, None]) & (pair_order[None, :] < pair_order[:, None])
    slot_rank = jnp.sum(earlier.astype(jnp.int32), axis=1)
    slot_key = flat_ids * capacity + slot_rank
    slot_match = slot_key[None, :] == jnp.arange(slot_count, dtype=jnp.int32)[:, None]
    filled = jnp.any(slot_match, axis=1)
    source_pair = jnp.sum(jnp.where(slot_match, pair_order[None, :], 0), axis=1)
    send_x = jnp.where(
        filled[:, None], layer_input[source_pair // top_count], jnp.zeros((), jnp.bfloat16)
    )
    send_grad = jnp.where(filled[:, None], scaled[source_pair], jnp.zeros((), jnp.bfloat16))
    recv_x, recv_grad = (
        lax.all_to_all(
            send_x.reshape(devices, capacity, model_width),
            ("grp", "mem"),
            split_axis=0,
            concat_axis=0,
            tiled=True,
        ),
        lax.all_to_all(
            send_grad.reshape(devices, capacity, model_width),
            ("grp", "mem"),
            split_axis=0,
            concat_axis=0,
            tiled=True,
        ),
    )
    rows_x = recv_x.reshape(slot_count, model_width)
    rows_grad = recv_grad.reshape(slot_count, model_width)
    gate_w = w_gate[0]
    up_w = w_up[0]
    down_w = w_down[0]
    gate_pre = jnp.dot(rows_x, gate_w, preferred_element_type=jnp.float32)
    up_pre = jnp.dot(rows_x, up_w, preferred_element_type=jnp.float32)
    sigmoid_gate = jax.nn.sigmoid(gate_pre)
    activity = gate_pre * sigmoid_gate
    hidden = (activity * up_pre).astype(jnp.bfloat16)
    hidden_grad = jnp.dot(rows_grad, down_w.T, preferred_element_type=jnp.float32)
    up_grad = (hidden_grad * activity).astype(jnp.bfloat16)
    gate_grad = (
        hidden_grad * up_pre * sigmoid_gate * (1.0 + gate_pre * (1.0 - sigmoid_gate))
    ).astype(jnp.bfloat16)
    row_grad = (
        jnp.dot(gate_grad, gate_w.T, preferred_element_type=jnp.float32)
        + jnp.dot(up_grad, up_w.T, preferred_element_type=jnp.float32)
    ).astype(jnp.bfloat16)
    returned = lax.all_to_all(
        row_grad.reshape(devices, capacity, model_width),
        ("grp", "mem"),
        split_axis=0,
        concat_axis=0,
        tiled=True,
    )
    down_wgrad = jnp.dot(hidden.T, rows_grad, preferred_element_type=jnp.float32).astype(
        jnp.bfloat16
    )
    gate_wgrad = jnp.dot(rows_x.T, gate_grad, preferred_element_type=jnp.float32).astype(
        jnp.bfloat16
    )
    up_wgrad = jnp.dot(rows_x.T, up_grad, preferred_element_type=jnp.float32).astype(jnp.bfloat16)
    back_rows = returned.reshape(slot_count, model_width)
    pair_rows = back_rows[slot_key].reshape(tok_rows, top_count, model_width)
    input_grad = jnp.sum(pair_rows.astype(jnp.float32), axis=1).astype(jnp.bfloat16)
    return (input_grad, gate_wgrad[None], up_wgrad[None], down_wgrad[None])


TN = (((0,), (0,)), ((), ()))
NT = (((1,), (1,)), ((), ()))


def ring_order(count):
    return list(range(0, count, 2)) + list(reversed(range(1, count, 2)))


def mm(a, b, dims=(((1,), (0,)), ((), ()))):
    return lax.dot_general(a, b, dims, preferred_element_type=jnp.float32)


def ring_plan(layer_input, output_grad, expert_ids, route_ints, w_gate, w_up, w_down):
    groups = lax.axis_size("grp")
    members = lax.axis_size("mem")
    tok_rows, model_width = layer_input.shape
    width = w_gate.shape[2]
    span = members * width
    order = ring_order(groups)
    full_steps = (groups - 1) // 2
    has_far = groups % 2 == 0 and groups > 1

    def at_distance(k):
        return [(order[i], order[(i + k) % groups]) for i in range(groups)]

    def shift(array, k):
        return lax.ppermute(array, "grp", at_distance(k))

    def member_shift(array, step):
        return lax.ppermute(array, "mem", [(m, (m + step) % members) for m in range(members)])

    half = tok_rows // 2
    low, high = slice(0, half), slice(half, tok_rows)
    rg, lx = output_grad, layer_input
    rx = {high: layer_input[high], low: layer_input[low]}
    lg = {low: output_grad[low], high: output_grad[high]}
    from_left, from_right = [], []
    for k in range(1, full_steps + 1):
        rg, lx = shift(rg, 1), shift(lx, -1)
        rx = {high: shift(rx[high], 1), low: shift(rx[low], 1)}
        lg = {low: shift(lg[low], -1), high: shift(lg[high], -1)}
        from_left.append((rx, {low: rg[low], high: rg[high]}))
        from_right.append(({low: lx[low], high: lx[high]}, lg, lx))
        from_left[-1] += (rg,)
    far = (shift(lx, -1), shift(rg, 1)) if has_far else None

    quotas = route_ints.astype(jnp.float32)
    route_ratio = quotas / jnp.sum(quotas, axis=1, keepdims=True)
    group_at = jnp.array(
        [[order[(order.index(g) + k) % groups] for k in range(groups)] for g in range(groups)],
        jnp.int32,
    )
    mine = jnp.arange(groups, dtype=jnp.int32)[:, None] == lax.axis_index("grp")
    chip = jnp.sum(jnp.where(mine, group_at, 0), axis=0)
    core = (lax.axis_index("mem") + jnp.arange(members, dtype=jnp.int32)) % members
    expert = chip[:, None] * members + core[None, :]
    chosen = expert_ids[None, None, :, :] == expert[:, :, None, None]
    outgoing = jnp.sum(jnp.where(chosen, route_ratio[None, None], 0.0), axis=3)

    distances = [d for k in range(1, full_steps + 1) for d in (k, -k)] + [groups // 2] * has_far
    blocks = {d: outgoing[d % groups] for d in distances}
    for bit in range((groups // 2).bit_length()):
        for sign in (1, -1):
            going = [d for d in distances if d * sign > 0 and abs(d) >> bit & 1]
            if not going:
                continue
            packed = jnp.concatenate([blocks[d] for d in going], axis=0)
            moved = shift(packed, sign << bit)
            for i, d in enumerate(going):
                blocks[d] = moved[i * members : (i + 1) * members]

    def ratio_from(distance):
        return blocks[-distance]

    gates, ups, downs = [w_gate[0]], [w_up[0]], [w_down[0]]
    for k in range(1, members):
        gates.append(member_shift(w_gate[0], members - k))
        ups.append(member_shift(w_up[0], members - k))
        downs.append(member_shift(w_down[0], members - k))
    gate_w = jnp.concatenate(gates, axis=1)
    up_w = jnp.concatenate(ups, axis=1)
    down_t = with_layout_constraint(
        jnp.concatenate(downs, axis=0).T, Layout(major_to_minor=(0, 1))
    )
    column = jnp.arange(span, dtype=jnp.int32)[None, :] // width

    def piece(x, og, ratio):
        r = ratio[:, 0:1]
        for m in range(1, members):
            r = jnp.where(column == m, ratio[:, m : m + 1], r)
        gate, up = mm(x, gate_w), mm(x, up_w)
        s = jax.nn.sigmoid(gate)
        act = gate * s
        hidden = (act * up * r).astype(jnp.bfloat16)
        hg = r * mm(og, down_t)
        ug = (hg * act).astype(jnp.bfloat16)
        gg = (hg * up * s * (1.0 + gate * (1.0 - s))).astype(jnp.bfloat16)
        part = mm(gg, gate_w, NT) + mm(ug, up_w, NT)
        return part, gg, ug, hidden

    kept = []

    def step_piece(xs, ogs, ratios, apart=False):
        x, og = jnp.concatenate(xs, axis=0), jnp.concatenate(ogs, axis=0)
        if apart:
            x, og = lax.optimization_barrier((x, og))
        ratio = jnp.concatenate(ratios, axis=1).T
        if kept:
            ratio = lax.optimization_barrier((ratio, kept[-1][2]))[0]
        part, *rest = piece(x, og, ratio)
        kept.append((x, og, *rest))
        return part.astype(jnp.bfloat16)

    parts = {}
    for k in range(1, full_steps):
        lefts, rights = from_left[k - 1], from_right[k - 1]
        xs = [lefts[0][low], lefts[0][high], rights[2]]
        ogs = [lefts[2], rights[1][low], rights[1][high]]
        ratio = [ratio_from(-k), ratio_from(k)]
        if k == 1:
            xs, ogs, ratio = xs + [layer_input], ogs + [output_grad], ratio + [outgoing[0]]
        part = step_piece(xs, ogs, ratio)
        parts[k] = [
            {rows: part[at + rows.start : at + rows.stop] for rows in (low, high)}
            for at in (0, tok_rows)
        ]
        if k == 1:
            own_part = part[2 * tok_rows :]
    if full_steps < 2:
        own_part = step_piece([layer_input], [output_grad], [outgoing[0]])

    def far_piece():
        return step_piece([far[0]], [far[1]], [blocks[groups // 2]]) if has_far else None

    far_part = far_piece()
    if full_steps:
        k = full_steps
        lefts, rights = from_left[k - 1], from_right[k - 1]
        parts[k] = [{}, {}]
        for one, two in ((high, low), (low, high)):
            ratio = [ratio_from(-k)[:, one], ratio_from(k)[:, two]]
            part = step_piece(
                [lefts[0][one], rights[0][two]], [lefts[1][one], rights[1][two]], ratio, apart=True
            )
            parts[k][0][one], parts[k][1][two] = part[:half], part[half:]

    def join(moved, part):
        return (moved.astype(jnp.float32) + part.astype(jnp.float32)).astype(jnp.bfloat16)

    def send(pair):
        return shift(pair[0], -1), shift(pair[1], 1)

    def parts_at(k, rows):
        return parts[k][0][rows[0]], parts[k][1][rows[1]]

    long_rows, short_rows = (low, high), (high, low)
    long_way = short_way = before = None

    def gated(pair):
        return pair if before is None else lax.optimization_barrier((pair, before))[0]

    if has_far:
        long_way = send((far_part[low], far_part[high]))
    for k in reversed(range(1, full_steps + 1)):
        sums = parts_at(k, short_rows)
        if short_way is not None:
            sums = before = tuple(map(join, short_way, gated(sums)))
        short_way = send(sums)
        sums = parts_at(k, long_rows)
        if long_way is not None:
            sums = before = tuple(map(join, long_way, gated(sums)))
        long_way = send(sums)
    back_low = [long_way and long_way[0], short_way and short_way[1]]
    back_high = [long_way and long_way[1], short_way and short_way[0]]

    def closing(rows, returned):
        total = own_part[rows].astype(jnp.float32)
        for piece_back in returned:
            if piece_back is not None:
                total = total + piece_back.astype(jnp.float32)
        return total.astype(jnp.bfloat16)

    input_grad = jnp.zeros((tok_rows, model_width), jnp.bfloat16)
    input_grad = lax.dynamic_update_slice(input_grad, closing(low, back_low), (0, 0))
    input_grad = lax.dynamic_update_slice(input_grad, closing(high, back_high), (half, 0))

    x_all, og_all, gg_all, ug_all, hidden_all = (
        jnp.concatenate([k[i] for k in kept], axis=0) for i in range(5)
    )

    def member_sum(product, axis):
        both = lax.optimization_barrier(product.astype(jnp.bfloat16))
        blocks = jnp.split(both, members, axis=axis)
        moved = [member_shift(blocks[k], k) for k in range(1, members)]
        total = sum(block.astype(jnp.float32) for block in [blocks[0], *moved])
        return total.astype(jnp.bfloat16)[None]

    gate_p = mm(x_all, gg_all, TN)
    up_p = mm(x_all, ug_all, TN)
    down_p = mm(hidden_all, og_all, TN)
    gate_g = member_sum(gate_p, 1)
    up_g = member_sum(up_p, 1)
    down_g = member_sum(down_p, 0)
    return (input_grad, gate_g, up_g, down_g)


def local(layer_input, output_grad, expert_ids, route_ints, w_gate, w_up, w_down):
    devices = lax.axis_size("grp") * lax.axis_size("mem")
    tok_rows, top_count = expert_ids.shape
    capacity = max(2, 9 * tok_rows * top_count // (8 * devices))
    plan = ring_plan if tok_rows <= 2 * capacity else exchange_plan
    return plan(layer_input, output_grad, expert_ids, route_ints, w_gate, w_up, w_down)


def solution(mesh):
    return jax.shard_map(
        local,
        mesh=mesh,
        in_specs=(
            P(("rep", "grp", "mem"), None),
            P(("rep", "grp", "mem"), None),
            P(("rep", "grp", "mem"), None),
            P(("rep", "grp", "mem"), None),
            P(("grp", "mem"), None, None),
            P(("grp", "mem"), None, None),
            P(("grp", "mem"), None, None),
        ),
        out_specs=(
            P(("rep", "grp", "mem"), None),
            P(("rep", "grp", "mem"), None, None),
            P(("rep", "grp", "mem"), None, None),
            P(("rep", "grp", "mem"), None, None),
        ),
        check_vma=False,
    )
```

```python
import jax
import jax.numpy as jnp
from jax import lax
from jax.experimental.layout import Layout, with_layout_constraint
from jax.sharding import PartitionSpec as P


def exchange_plan(layer_input, output_grad, expert_ids, route_ints, w_gate, w_up, w_down):
    devices = lax.axis_size("grp") * lax.axis_size("mem")
    tok_rows = layer_input.shape[0]
    model_width = layer_input.shape[1]
    top_count = expert_ids.shape[1]
    pair_count = tok_rows * top_count
    capacity = max(2, 9 * tok_rows * top_count // (8 * devices))
    slot_count = devices * capacity
    quotas = route_ints.astype(jnp.float32)
    route_ratio = quotas / jnp.sum(quotas, axis=1, keepdims=True)
    scaled = (route_ratio[:, :, None] * output_grad.astype(jnp.float32)[:, None, :]).astype(
        jnp.bfloat16
    )
    scaled = scaled.reshape(pair_count, model_width)
    flat_ids = expert_ids.reshape(pair_count)
    pair_order = jnp.arange(pair_count, dtype=jnp.int32)
    earlier = (flat_ids[None, :] == flat_ids[:, None]) & (pair_order[None, :] < pair_order[:, None])
    slot_rank = jnp.sum(earlier.astype(jnp.int32), axis=1)
    slot_key = flat_ids * capacity + slot_rank
    slot_match = slot_key[None, :] == jnp.arange(slot_count, dtype=jnp.int32)[:, None]
    filled = jnp.any(slot_match, axis=1)
    source_pair = jnp.sum(jnp.where(slot_match, pair_order[None, :], 0), axis=1)
    send_x = jnp.where(
        filled[:, None], layer_input[source_pair // top_count], jnp.zeros((), jnp.bfloat16)
    )
    send_grad = jnp.where(filled[:, None], scaled[source_pair], jnp.zeros((), jnp.bfloat16))
    recv_x, recv_grad = (
        lax.all_to_all(
            send_x.reshape(devices, capacity, model_width),
            ("grp", "mem"),
            split_axis=0,
            concat_axis=0,
            tiled=True,
        ),
        lax.all_to_all(
            send_grad.reshape(devices, capacity, model_width),
            ("grp", "mem"),
            split_axis=0,
            concat_axis=0,
            tiled=True,
        ),
    )
    rows_x = recv_x.reshape(slot_count, model_width)
    rows_grad = recv_grad.reshape(slot_count, model_width)
    gate_w = w_gate[0]
    up_w = w_up[0]
    down_w = w_down[0]
    gate_pre = jnp.dot(rows_x, gate_w, preferred_element_type=jnp.float32)
    up_pre = jnp.dot(rows_x, up_w, preferred_element_type=jnp.float32)
    sigmoid_gate = jax.nn.sigmoid(gate_pre)
    activity = gate_pre * sigmoid_gate
    hidden = (activity * up_pre).astype(jnp.bfloat16)
    hidden_grad = jnp.dot(rows_grad, down_w.T, preferred_element_type=jnp.float32)
    up_grad = (hidden_grad * activity).astype(jnp.bfloat16)
    gate_grad = (
        hidden_grad * up_pre * sigmoid_gate * (1.0 + gate_pre * (1.0 - sigmoid_gate))
    ).astype(jnp.bfloat16)
    row_grad = (
        jnp.dot(gate_grad, gate_w.T, preferred_element_type=jnp.float32)
        + jnp.dot(up_grad, up_w.T, preferred_element_type=jnp.float32)
    ).astype(jnp.bfloat16)
    returned = lax.all_to_all(
        row_grad.reshape(devices, capacity, model_width),
        ("grp", "mem"),
        split_axis=0,
        concat_axis=0,
        tiled=True,
    )
    down_wgrad = jnp.dot(hidden.T, rows_grad, preferred_element_type=jnp.float32).astype(
        jnp.bfloat16
    )
    gate_wgrad = jnp.dot(rows_x.T, gate_grad, preferred_element_type=jnp.float32).astype(
        jnp.bfloat16
    )
    up_wgrad = jnp.dot(rows_x.T, up_grad, preferred_element_type=jnp.float32).astype(jnp.bfloat16)
    back_rows = returned.reshape(slot_count, model_width)
    pair_rows = back_rows[slot_key].reshape(tok_rows, top_count, model_width)
    input_grad = jnp.sum(pair_rows.astype(jnp.float32), axis=1).astype(jnp.bfloat16)
    return (input_grad, gate_wgrad[None], up_wgrad[None], down_wgrad[None])


TN = (((0,), (0,)), ((), ()))
NT = (((1,), (1,)), ((), ()))


def ring_order(count):
    return list(range(0, count, 2)) + list(reversed(range(1, count, 2)))


def mm(a, b, dims=(((1,), (0,)), ((), ()))):
    return lax.dot_general(a, b, dims, preferred_element_type=jnp.float32)


def ring_plan(layer_input, output_grad, expert_ids, route_ints, w_gate, w_up, w_down):
    groups = lax.axis_size("grp")
    members = lax.axis_size("mem")
    tok_rows, _ = layer_input.shape
    width = w_gate.shape[2]
    span = members * width
    order = ring_order(groups)
    full_steps = (groups - 1) // 2
    has_far = groups % 2 == 0 and groups > 1

    def at_distance(k):
        return [(order[i], order[(i + k) % groups]) for i in range(groups)]

    def shift(array, k):
        return lax.ppermute(array, "grp", at_distance(k))

    def member_shift(array, step):
        return lax.ppermute(array, "mem", [(m, (m + step) % members) for m in range(members)])

    half = tok_rows // 2
    low, high = slice(0, half), slice(half, tok_rows)
    rg, lx = output_grad, layer_input
    rx = {high: layer_input[high], low: layer_input[low]}
    lg = {low: output_grad[low], high: output_grad[high]}
    from_left, from_right = [], []
    for k in range(1, full_steps + 1):
        rg, lx = shift(rg, 1), shift(lx, -1)
        rx = {high: shift(rx[high], 1), low: shift(rx[low], 1)}
        lg = {low: shift(lg[low], -1), high: shift(lg[high], -1)}
        from_left.append((rx, {low: rg[low], high: rg[high]}))
        from_right.append(({low: lx[low], high: lx[high]}, lg, lx))
        from_left[-1] += (rg,)
    far = (shift(lx, -1), shift(rg, 1)) if has_far else None

    quotas = route_ints.astype(jnp.float32)
    route_ratio = quotas / jnp.sum(quotas, axis=1, keepdims=True)
    group_at = jnp.array(
        [[order[(order.index(g) + k) % groups] for k in range(groups)] for g in range(groups)],
        jnp.int32,
    )
    mine = jnp.arange(groups, dtype=jnp.int32)[:, None] == lax.axis_index("grp")
    chip = jnp.sum(jnp.where(mine, group_at, 0), axis=0)
    core = (lax.axis_index("mem") + jnp.arange(members, dtype=jnp.int32)) % members
    expert = chip[:, None] * members + core[None, :]
    chosen = expert_ids[None, None, :, :] == expert[:, :, None, None]
    outgoing = jnp.sum(jnp.where(chosen, route_ratio[None, None], 0.0), axis=3)

    distances = [d for k in range(1, full_steps + 1) for d in (k, -k)] + [groups // 2] * has_far
    blocks = {d: outgoing[d % groups] for d in distances}
    for bit in range((groups // 2).bit_length()):
        for sign in (1, -1):
            going = [d for d in distances if d * sign > 0 and abs(d) >> bit & 1]
            if not going:
                continue
            packed = jnp.concatenate([blocks[d] for d in going], axis=0)
            moved = shift(packed, sign << bit)
            for i, d in enumerate(going):
                blocks[d] = moved[i * members : (i + 1) * members]

    def ratio_from(distance):
        return blocks[-distance]

    gates, ups, downs = [w_gate[0]], [w_up[0]], [w_down[0]]
    for k in range(1, members):
        gates.append(member_shift(w_gate[0], members - k))
        ups.append(member_shift(w_up[0], members - k))
        downs.append(member_shift(w_down[0], members - k))
    gate_w = jnp.concatenate(gates, axis=1)
    up_w = jnp.concatenate(ups, axis=1)
    down_t = with_layout_constraint(
        jnp.concatenate(downs, axis=0).T, Layout(major_to_minor=(0, 1))
    )
    column = jnp.arange(span, dtype=jnp.int32)[None, :] // width

    def piece(x, og, ratio):
        r = ratio[:, 0:1]
        for m in range(1, members):
            r = jnp.where(column == m, ratio[:, m : m + 1], r)
        gate, up = mm(x, gate_w), mm(x, up_w)
        s = jax.nn.sigmoid(gate)
        act = gate * s
        hidden = (act * up * r).astype(jnp.bfloat16)
        hg = r * mm(og, down_t)
        ug = (hg * act).astype(jnp.bfloat16)
        gg = (hg * up * s * (1.0 + gate * (1.0 - s))).astype(jnp.bfloat16)
        part = mm(gg, gate_w, NT) + mm(ug, up_w, NT)
        return part, gg, ug, hidden

    kept = []

    def step_piece(xs, ogs, ratios, apart=False):
        x, og = jnp.concatenate(xs, axis=0), jnp.concatenate(ogs, axis=0)
        if apart:
            x, og = lax.optimization_barrier((x, og))
        ratio = jnp.concatenate(ratios, axis=1).T
        if kept:
            ratio = lax.optimization_barrier((ratio, kept[-1][2]))[0]
        part, *rest = piece(x, og, ratio)
        kept.append((x, og, *rest))
        return part.astype(jnp.bfloat16)

    parts = {}
    for k in range(1, full_steps):
        lefts, rights = from_left[k - 1], from_right[k - 1]
        xs = [lefts[0][low], lefts[0][high], rights[2]]
        ogs = [lefts[2], rights[1][low], rights[1][high]]
        ratio = [ratio_from(-k), ratio_from(k)]
        if k == 1:
            xs, ogs, ratio = xs + [layer_input], ogs + [output_grad], ratio + [outgoing[0]]
        part = step_piece(xs, ogs, ratio)
        parts[k] = [
            {rows: part[at + rows.start : at + rows.stop] for rows in (low, high)}
            for at in (0, tok_rows)
        ]
        if k == 1:
            own_part = part[2 * tok_rows :]
    if full_steps < 2:
        own_part = step_piece([layer_input], [output_grad], [outgoing[0]])

    def far_piece():
        return step_piece([far[0]], [far[1]], [blocks[groups // 2]]) if has_far else None

    far_part = far_piece()
    if full_steps:
        k = full_steps
        lefts, rights = from_left[k - 1], from_right[k - 1]
        parts[k] = [{}, {}]
        for one, two in ((high, low), (low, high)):
            ratio = [ratio_from(-k)[:, one], ratio_from(k)[:, two]]
            part = step_piece(
                [lefts[0][one], rights[0][two]], [lefts[1][one], rights[1][two]], ratio, apart=True
            )
            parts[k][0][one], parts[k][1][two] = part[:half], part[half:]

    def join(moved, part):
        return (moved.astype(jnp.float32) + part.astype(jnp.float32)).astype(jnp.bfloat16)

    def send(pair):
        return shift(pair[0], -1), shift(pair[1], 1)

    def parts_at(k, rows):
        return parts[k][0][rows[0]], parts[k][1][rows[1]]

    long_rows, short_rows = (low, high), (high, low)
    long_way = short_way = before = None

    def gated(pair):
        return pair if before is None else lax.optimization_barrier((pair, before))[0]

    if has_far:
        long_way = send((far_part[low], far_part[high]))
    for k in reversed(range(1, full_steps + 1)):
        sums = parts_at(k, short_rows)
        if short_way is not None:
            sums = before = tuple(map(join, short_way, gated(sums)))
        short_way = send(sums)
        sums = parts_at(k, long_rows)
        if long_way is not None:
            sums = before = tuple(map(join, long_way, gated(sums)))
        long_way = send(sums)

    def spread(piece_back, rows):
        edges = [(rows.start, tok_rows - rows.stop, 0), (0, 0, 0)]
        return lax.pad(piece_back, jnp.zeros((), jnp.bfloat16), edges).astype(jnp.float32)

    total = own_part.astype(jnp.float32)
    if short_way is not None:
        total = total + spread(short_way[0], high) + spread(short_way[1], low)
        total = lax.optimization_barrier(total)
    if long_way is not None:
        total = total + spread(long_way[0], low) + spread(long_way[1], high)
    input_grad = total.astype(jnp.bfloat16)

    x_all, og_all, gg_all, ug_all, hidden_all = (
        jnp.concatenate([k[i] for k in kept], axis=0) for i in range(5)
    )

    def member_sum(product, axis):
        both = lax.optimization_barrier(product.astype(jnp.bfloat16))
        blocks = jnp.split(both, members, axis=axis)
        moved = [member_shift(blocks[k], k) for k in range(1, members)]
        total = sum(block.astype(jnp.float32) for block in [blocks[0], *moved])
        return total.astype(jnp.bfloat16)[None]

    gate_p = mm(x_all, gg_all, TN)
    up_p = mm(x_all, ug_all, TN)
    down_p = mm(hidden_all, og_all, TN)
    gate_g = member_sum(gate_p, 1)
    up_g = member_sum(up_p, 1)
    down_g = member_sum(down_p, 0)
    return (input_grad, gate_g, up_g, down_g)


def local(layer_input, output_grad, expert_ids, route_ints, w_gate, w_up, w_down):
    devices = lax.axis_size("grp") * lax.axis_size("mem")
    tok_rows, top_count = expert_ids.shape
    capacity = max(2, 9 * tok_rows * top_count // (8 * devices))
    plan = ring_plan if tok_rows <= 2 * capacity else exchange_plan
    return plan(layer_input, output_grad, expert_ids, route_ints, w_gate, w_up, w_down)


def solution(mesh):
    return jax.shard_map(
        local,
        mesh=mesh,
        in_specs=(
            P(("rep", "grp", "mem"), None),
            P(("rep", "grp", "mem"), None),
            P(("rep", "grp", "mem"), None),
            P(("rep", "grp", "mem"), None),
            P(("grp", "mem"), None, None),
            P(("grp", "mem"), None, None),
            P(("grp", "mem"), None, None),
        ),
        out_specs=(
            P(("rep", "grp", "mem"), None),
            P(("rep", "grp", "mem"), None, None),
            P(("rep", "grp", "mem"), None, None),
            P(("rep", "grp", "mem"), None, None),
        ),
        check_vma=False,
    )
```
